32 devices in a mesh: gx: 4 (over x, core), gy: 8 (over z, y).
Axes of the slice: x: 2, y: 2, z: 4, core: 2. Of those that a mesh axis runs over, the one named last changes fastest.
Arguments:
- queries: bfloat16 [256, 2560], P('gx'), may hold values from -8 to 8
- token_key_value: bfloat16 [256, 1024], P('gx'), may hold values from -6 to 6
- group_cached_keys: bfloat16 [4, 32768, 512], P('gx', 'gy'), may hold values from -8 to 8
- group_cached_values: bfloat16 [4, 32768, 512], P('gx', 'gy'), may hold values from -6 to 6
- owners: int32 [4, 32768], P('gx', 'gy'), may hold values from 0 to 63, never falling along the last dimension, each value on 1 to 16384 neighbouring positions
- out_weight: bfloat16 [2560, 2560], P(None, 'gy'), may hold values from -0.125 to 0.125
- residual: bfloat16 [256, 2560], P('gx', 'gy'), may hold values from -6 to 6
- norm_gain: bfloat16 [2560], P('gy'), may hold values from 0.099609375 to 1.8984375
- expert_ids: int32 [256, 6], replicated, may hold values from 0 to 63, all different within a row; in each aligned block of 64 rows (0 to 63, 64 to 127, ...) at most 12 rows name the same one
- gate_logits: float32 [256, 6], replicated, may hold values from -0.5 to 0.5
- w_gate_up: bfloat16 [64, 2560, 3072], P('gx', 'gy'), may hold values from -0.125 to 0.125
- w_down: bfloat16 [64, 1536, 2560], P('gx', None, 'gy'), may hold values from -0.15625 to 0.15625
Outputs:
- layer_out: float32 [256, 2560], P('gx', 'gy')
The draws below stay inside these ranges and needn't reach their ends.
Inputs may be any that keep to these rules, and one draw needn't show every extreme that they name: `owners`: each request's positions form one run; every request owns at least one position and at most 16384, and some request owns exactly 16384. `expert_ids`: within each group of 64 requests no expert is named by more than 12 requests, a bound that some block reaches.
All inputs are finite; a program needn't handle non-finite values.
Results may differ from the reference program's by a relative error of at most 0.0075.
Values may be sent and summed in bfloat16 or wider, within the bound.
No kernel may reach another device: no remote copies, remote signals or barrier semaphores. Data moves between devices by JAX's collectives and lax.ppermute only.
A program may use at most 192 MiB of HBM per device.

```python
import math
import jax
import jax.numpy as jnp
import numpy as np
from jax import lax

D = 2560
QUERY_HEADS = 20
KEY_VALUE_HEADS = 4
HEAD_SIZE = 128
E = 64
F = 1536
TOPK = 6
GROUP_REQUESTS = 64
QD = 2560
KD = 512
REQUEST_GROUPS = 4
B = 256
CACHED_POSITIONS = 32768
LMOST = 16384
CAPS = 12
N_GX = 4


def draw_queries(key, part):
    random_root_key = jax.random.fold_in(key, 11)
    value_rows = 2.5 * jax.random.normal(jax.random.fold_in(random_root_key, 3), (B, QUERY_HEADS, HEAD_SIZE), jnp.float32)
    return jnp.clip(value_rows, -8.0, 8.0).reshape(B, QD).astype(jnp.bfloat16)


def draw_group_cached_keys(key, part):
    random_root_key = jax.random.fold_in(key, 23)
    value_rows = jax.random.normal(jax.random.fold_in(random_root_key, 3), (REQUEST_GROUPS, CACHED_POSITIONS, KEY_VALUE_HEADS, HEAD_SIZE), jnp.float32)
    return jnp.clip(value_rows, -8.0, 8.0).reshape(REQUEST_GROUPS, CACHED_POSITIONS, KD).astype(jnp.bfloat16)


def draw_residual(key, part):
    random_root_key = jax.random.fold_in(key, 37)
    position = jnp.arange(D, dtype=jnp.float32) / max(D - 1, 1)
    base_values = jax.random.normal(jax.random.fold_in(random_root_key, 3), (B, D), jnp.float32)
    column_scale = 0.05 * jnp.exp(position * jnp.log(20.0))
    row_scale = jnp.exp(jax.random.uniform(jax.random.fold_in(random_root_key, 4), (B, 1), jnp.float32, jnp.log(0.5), jnp.log(2.0)))
    value_rows = base_values * row_scale * column_scale[None, :]
    return jnp.clip(value_rows, -6.0, 6.0).astype(jnp.bfloat16)


def steps_of(key, shape, split, smallest, high):
    def one(axis_at, parts):
        draws = jax.random.uniform(jax.random.fold_in(jax.random.fold_in(key, 6), axis_at), (parts,), jnp.float32, smallest / len(split), high / len(split))
        return jnp.repeat(jnp.exp(draws), shape[axis_at] // parts).reshape((-1,) + (1,) * (len(shape) - axis_at - 1))

    gain = one(*split[0])
    for cut in split[1:]:
        gain = gain * one(*cut)
    return gain


def length_profile(count, total, most, slope):
    weights = [(1 << 20) // math.isqrt(standing ** slope) + 1 for standing in range(2, count + 1)]
    surplus, holding = total - most - (count - 1), [1] * (count - 1)
    while surplus > 0:
        free = [i for i in range(count - 1) if holding[i] < most]
        pool, budget = sum([weights[i] for i in free]), surplus
        for i in free:
            more = min(most - holding[i], max(1, budget * weights[i] // pool), surplus)
            holding[i] = holding[i] + more
            surplus = surplus - more
    return np.array([most] + holding)


def ragged(stream_key, number_of, total, limit, lean):
    if number_of == 2:
        one = jax.random.randint(stream_key, (), max(1, total - limit), min(limit, total - 1) + 1)
        return jnp.stack([one, total - one])
    lengths = jnp.asarray(length_profile(number_of, total, limit, lean), jnp.int32)
    pairs = (number_of - 1) // 2
    source_of, taker = lengths[1:1 + 2 * pairs:2], lengths[2:2 + 2 * pairs:2]
    margin = jnp.minimum(source_of - 1, limit - taker)
    moved = jax.random.randint(jax.random.fold_in(stream_key, 1), (pairs,), 0, 1 << 20) % (margin + 1)
    lengths = lengths.at[1:1 + 2 * pairs:2].set(source_of - moved).at[2:2 + 2 * pairs:2].set(taker + moved)
    return lengths[jax.random.permutation(jax.random.fold_in(stream_key, 2), number_of)]


def routed_block(rng, own, number, rows, count, top, bound, lean):
    sequence = jax.random.permutation(rng, count)
    heavy_load, common = portions_of(count, rows * top, bound, lean, True), portions_of(count, rows * top, bound, lean, False)
    places = jnp.arange(count)

    def named(sizes, rotation):
        used = int((sizes > 0).sum())
        fixed = max(1, used // 4)
        shifted = fixed + (places - fixed + rotation * (used - fixed)) % max(1, count - fixed)
        return jnp.zeros((count,), jnp.int32).at[sequence[jnp.where(places < fixed, places, shifted)]].set(jnp.asarray(sizes, jnp.int32))

    sizes = jnp.where(number % 4 == 0, named(heavy_load, number // 4), named(common, number - number // 4 - 1))
    mixed = jax.random.permutation(jax.random.fold_in(own, 3), count)
    donor, taker = mixed[0:count // 2 * 2:2], mixed[1:count // 2 * 2:2]
    margin = jnp.minimum(sizes[donor] - 1, bound - sizes[taker]) // 2
    margin = jnp.where((donor == sequence[0]) | (taker == sequence[0]) | (sizes[taker] == 0), 0, jnp.maximum(margin, 0))
    shifted = jax.random.randint(jax.random.fold_in(own, 4), (count // 2,), 0, 1 << 20) % (margin + 1)
    sizes = sizes.at[donor].add(-shifted).at[taker].add(shifted)
    items = jnp.searchsorted(jnp.cumsum(sizes), jnp.arange(rows * top), side="right").astype(jnp.int32)
    listing = items.reshape(top, rows).T
    listing = listing[jax.random.permutation(jax.random.fold_in(own, 1), rows)]
    rotation = jax.random.randint(jax.random.fold_in(own, 2), (rows, 1), 0, top)
    return jnp.take_along_axis(listing, (jnp.arange(top)[None, :] + rotation) % top, axis=1)


def portions_of(number_of, total, bound, skew, full):
    weights = [(1 << 20) // math.isqrt(rank ** skew) + 1 for rank in range(1, number_of + 1)]
    largest = bound if full else min(bound, max(-(-total // number_of), total * weights[0] // sum(weights)))
    least = 1 if total - largest >= number_of - 1 else 0
    counts, rest = [largest] + [least] * (number_of - 1), total - largest - least * (number_of - 1)
    while rest > 0:
        movable = [i for i in range(1, number_of) if counts[i] < largest] or [i for i in range(1, number_of) if counts[i] < bound]
        whole, remaining = sum([weights[i] for i in movable]), rest
        for i in movable:
            more = min(bound - counts[i], max(1, remaining * weights[i] // whole), rest)
            counts[i] = counts[i] + more
            rest = rest - more
    return np.array(counts)


def centred(own_key, shape, scale, limit, pieces=(), kind=jnp.bfloat16):
    result = scale * jax.random.normal(own_key, shape, jnp.float32)
    if pieces:
        result = result * steps_of(own_key, shape, pieces, -0.22, 0.18)
    return jnp.clip(result, -limit, limit).astype(kind)


def setup_inputs(seed: int = 0) -> dict:
    keys = jax.random.split(jax.random.key(seed), 13)
    queries = draw_queries(jax.random.fold_in(keys[12], 71), 0)
    token_key_value = centred(keys[1], (B, 2 * KD), 1.0, 6.0, ((0, 4),))
    group_cached_keys = draw_group_cached_keys(jax.random.fold_in(keys[12], 71), 0)
    group_cached_values = centred(keys[3], (REQUEST_GROUPS, CACHED_POSITIONS, KD), 1.0, 6.0, ((0, 4), (1, 8)))
    owners = jax.vmap(lambda own: jnp.searchsorted(jnp.cumsum(ragged(own, GROUP_REQUESTS, CACHED_POSITIONS, LMOST, 2)), jnp.arange(CACHED_POSITIONS), side="right"))(jax.random.split(keys[4], REQUEST_GROUPS)).reshape((REQUEST_GROUPS, CACHED_POSITIONS)).astype(jnp.int32)
    out_weight = centred(keys[5], (QD, D), QD ** -0.5, 0.125, ((1, 8),))
    residual = draw_residual(jax.random.fold_in(keys[12], 71), 0)
    norm_gain = jnp.clip(1.0 + 0.18 * jax.random.normal(keys[7], (D,), jnp.float32), 0.099609375, 1.8984375).astype(jnp.bfloat16)
    expert_ids_keys = jax.random.split(jax.random.fold_in(keys[8], 1), B // GROUP_REQUESTS)
    expert_ids_turns = jax.random.permutation(jax.random.fold_in(keys[8], 3), B // GROUP_REQUESTS)
    expert_ids = jax.vmap(lambda own, number: routed_block(jax.random.fold_in(keys[8], 2), own, number, GROUP_REQUESTS, E, TOPK, CAPS, 2))(expert_ids_keys, expert_ids_turns).reshape((B, TOPK))
    gate_logits = jnp.clip(jax.random.uniform(keys[9], (B, TOPK), jnp.float32, -0.5, 0.5), -0.5, 0.5)
    w_gate_up = centred(keys[10], (E, D, 2 * F), D ** -0.5, 0.125, ((0, 4), (1, 8)))
    w_down = centred(keys[11], (E, F, D), F ** -0.5, 0.15625, ((0, 4), (2, 8)))
    return dict(queries=queries, token_key_value=token_key_value, group_cached_keys=group_cached_keys, group_cached_values=group_cached_values, owners=owners, out_weight=out_weight, residual=residual, norm_gain=norm_gain, expert_ids=expert_ids, gate_logits=gate_logits, w_gate_up=w_gate_up, w_down=w_down)


norm_epsilon = 1e-05

def group_attention(group_queries, updated_group, group_keys, group_values, owner_group):
    query_heads_per_group = QUERY_HEADS // KEY_VALUE_HEADS
    key_value_width = KEY_VALUE_HEADS * HEAD_SIZE
    scaling = HEAD_SIZE ** (-0.5)
    query_head_rows = group_queries.astype(jnp.float32).reshape(GROUP_REQUESTS, KEY_VALUE_HEADS, query_heads_per_group, HEAD_SIZE)
    every_key = group_keys.astype(jnp.float32).reshape(CACHED_POSITIONS, KEY_VALUE_HEADS, HEAD_SIZE)
    every_value = group_values.astype(jnp.float32).reshape(CACHED_POSITIONS, KEY_VALUE_HEADS, HEAD_SIZE)
    appended_keys = updated_group[:, :key_value_width].astype(jnp.float32).reshape(GROUP_REQUESTS, KEY_VALUE_HEADS, HEAD_SIZE)
    appended_values = updated_group[:, key_value_width:].astype(jnp.float32).reshape(GROUP_REQUESTS, KEY_VALUE_HEADS, HEAD_SIZE)
    scores = jnp.einsum('tkgd,tkd->tkg', query_head_rows[owner_group], every_key) * scaling
    own_score = jnp.einsum('rkgd,rkd->rkg', query_head_rows, appended_keys) * scaling
    peak = jnp.maximum(jax.ops.segment_max(scores, owner_group, num_segments=GROUP_REQUESTS), own_score)
    probs = lax.optimization_barrier(jnp.exp(scores - peak[owner_group]).astype(jnp.bfloat16)).astype(jnp.float32)
    own_prob = lax.optimization_barrier(jnp.exp(own_score - peak).astype(jnp.bfloat16)).astype(jnp.float32)
    den = jax.ops.segment_sum(probs, owner_group, num_segments=GROUP_REQUESTS) + own_prob
    weighted = probs[..., None] * every_value[:, :, None, :]
    acc = jax.ops.segment_sum(weighted, owner_group, num_segments=GROUP_REQUESTS) + own_prob[..., None] * appended_values[:, :, None, :]
    return (acc / den[..., None]).astype(jnp.bfloat16).reshape(GROUP_REQUESTS, QUERY_HEADS * HEAD_SIZE)

def reference(queries, token_key_value, group_cached_keys, group_cached_values, owners, out_weight, residual, norm_gain, expert_ids, gate_logits, w_gate_up, w_down):

    def one_group(group_index):
        return group_attention(lax.dynamic_slice_in_dim(queries, group_index * GROUP_REQUESTS, GROUP_REQUESTS, 0), lax.dynamic_slice_in_dim(token_key_value, group_index * GROUP_REQUESTS, GROUP_REQUESTS, 0), group_cached_keys[group_index], group_cached_values[group_index], owners[group_index])
    attention = lax.map(one_group, jnp.arange(REQUEST_GROUPS, dtype=jnp.int32)).reshape(B, QUERY_HEADS * HEAD_SIZE)
    projected = jnp.dot(attention, out_weight, preferred_element_type=jnp.float32)
    hidden = (residual.astype(jnp.float32) + projected).astype(jnp.bfloat16)
    hidden_f = hidden.astype(jnp.float32)
    inv_rms = 1.0 / jnp.sqrt(lax.optimization_barrier(jnp.mean(hidden_f * hidden_f, axis=1)) + norm_epsilon)
    normed = (hidden_f * inv_rms[:, None] * norm_gain.astype(jnp.float32)[None, :]).astype(jnp.bfloat16)
    mixing = jax.nn.softmax(gate_logits.astype(jnp.float32), axis=-1)
    slot_total = N_GX * CAPS

    def expert_step(routed, expert):
        coefficient = lax.optimization_barrier(jnp.sum(jnp.where(expert_ids == expert, mixing, 0.0), axis=1))
        selected = jnp.any(expert_ids == expert, axis=1)
        row_order = jnp.argsort(jnp.where(selected, 0, 1).astype(jnp.int32), stable=True)[:slot_total].astype(jnp.int32)
        gate_up = jnp.dot(normed[row_order], w_gate_up[expert], preferred_element_type=jnp.float32)
        active = (jax.nn.silu(gate_up[:, :F]) * gate_up[:, F:]).astype(jnp.bfloat16)
        expert_out = jnp.dot(active, w_down[expert], preferred_element_type=jnp.float32).astype(jnp.bfloat16)
        update = coefficient[row_order][:, None] * expert_out.astype(jnp.float32)
        return (routed.at[row_order].add(update), None)
    routed = lax.scan(expert_step, jnp.zeros((B, D), jnp.float32), jnp.arange(E, dtype=jnp.int32))[0]
    return hidden_f + routed
```

```python
import functools

import jax
import jax.numpy as jnp
from jax import lax
from jax.experimental import pallas as pl
from jax.experimental.pallas import tpu as pltpu
from jax.sharding import PartitionSpec as P

D = 2560
QUERY_HEADS = 20
KEY_VALUE_HEADS = 4
HEAD_SIZE = 128
GROUP = QUERY_HEADS // KEY_VALUE_HEADS
E = 64
TOPK = 6
CAPS = 12

LOWEST = -1e30
EPSILON = 1e-05
SCALING = HEAD_SIZE ** (-0.5)
BLOCK = 512
ROWS = 16
ALIGN = 16
CHUNKS = 4
EXPERTS_PER_STEP = 4

f32 = jnp.float32
bf16 = jnp.bfloat16
VMEM_LIMIT = 56 * 1024 * 1024


def params(**more):
    return pltpu.CompilerParams(vmem_limit_bytes=VMEM_LIMIT, **more)


def whole(shape):
    return pl.BlockSpec(shape, lambda *_: (0,) * len(shape))


def attend_kernel(owner_s, q_ref, k_ref, v_ref, own_ref, out_ref, q_scr, m_scr, l_scr, acc_scr):
    step = pl.program_id(0)
    groups = q_scr.shape[0]
    block = k_ref.shape[1]

    @pl.when(step == 0)
    def _():
        for rg in range(groups):
            for c in range(KEY_VALUE_HEADS):
                for g in range(GROUP):
                    h = c * GROUP + g
                    q_scr[rg, c, g * ROWS : (g + 1) * ROWS, :] = q_ref[
                        rg * ROWS : (rg + 1) * ROWS, h * HEAD_SIZE : (h + 1) * HEAD_SIZE
                    ]
        m_scr[...] = jnp.full(m_scr.shape, LOWEST, f32)
        l_scr[...] = jnp.zeros(l_scr.shape, f32)
        acc_scr[...] = jnp.zeros(acc_scr.shape, f32)

    first = owner_s[step * block] // ROWS
    last = owner_s[step * block + block - 1] // ROWS

    def visit(rg, carry):
        ids = rg * ROWS + lax.broadcasted_iota(jnp.int32, (ROWS, block), 0)
        member = own_ref[0:1, :] == ids
        for c in range(KEY_VALUE_HEADS):
            lanes = slice(c * HEAD_SIZE, (c + 1) * HEAD_SIZE)
            keys = k_ref[0, :, lanes]
            s = (
                lax.dot_general(
                    q_scr[rg, c], keys, (((1,), (1,)), ((), ())), preferred_element_type=f32
                )
                * SCALING
            )
            s = jnp.where(member[None], s.reshape(GROUP, ROWS, block), LOWEST)
            s = s.reshape(GROUP * ROWS, block)
            m_old = m_scr[rg, c]
            m_new = jnp.maximum(m_old, jnp.max(s, axis=1, keepdims=True))
            alpha = jnp.exp(m_old - m_new)
            p = jnp.exp(s - m_new[:, :1]).astype(bf16)
            l_scr[rg, c] = l_scr[rg, c] * alpha + jnp.sum(p.astype(f32), axis=1, keepdims=True)
            acc_scr[rg, c] = acc_scr[rg, c] * alpha + jnp.dot(
                p, v_ref[0, :, lanes], preferred_element_type=f32
            )
            m_scr[rg, c] = m_new
        return carry

    lax.fori_loop(first, last + 1, visit, 0)

    @pl.when(step == pl.num_programs(0) - 1)
    def _():
        width = QUERY_HEADS * HEAD_SIZE
        lane = lax.broadcasted_iota(jnp.int32, (ROWS, 128), 1)
        piece = lane % 3
        per = out_ref.shape[1]
        for rg in range(groups):

            def put(value, lanes):
                if per >= ROWS:
                    at = rg * ROWS
                    out_ref[at // per, at % per : at % per + ROWS, lanes] = value.astype(bf16)
                else:
                    for i in range(ROWS // per):
                        out_ref[(rg * ROWS) // per + i, :, lanes] = value[
                            i * per : (i + 1) * per
                        ].astype(bf16)

            tail = jnp.zeros((ROWS, 128), f32)
            for c in range(KEY_VALUE_HEADS):
                for g in range(GROUP):
                    h = c * GROUP + g
                    rows = slice(g * ROWS, (g + 1) * ROWS)
                    m = m_scr[rg, c, rows, :]
                    l = l_scr[rg, c, rows, :]
                    tail = jnp.where(lane // 6 == h, jnp.where(lane % 6 < 3, m, l), tail)
                    put(
                        acc_scr[rg, c, rows, :] / jnp.maximum(l, 1e-30),
                        slice(h * HEAD_SIZE, (h + 1) * HEAD_SIZE),
                    )
            high = tail.astype(bf16).astype(f32)
            rest = tail - high
            middle = rest.astype(bf16).astype(f32)
            low = (rest - middle).astype(bf16).astype(f32)
            put(
                jnp.where(piece == 0, high, jnp.where(piece == 1, middle, low)),
                slice(width, width + 128),
            )


def attend_local(queries, keys, values, owners, parts):
    rows, width = queries.shape
    positions, kv = keys.shape[1:]
    block = min(BLOCK, positions)
    groups = rows // ROWS
    state = (groups, KEY_VALUE_HEADS, GROUP * ROWS, 128)
    out = jax.ShapeDtypeStruct((parts, rows // parts, width + 128), bf16)
    return pl.pallas_call(
        attend_kernel,
        out_shape=out,
        grid_spec=pltpu.PrefetchScalarGridSpec(
            num_scalar_prefetch=1,
            grid=(positions // block,),
            in_specs=[
                whole((rows, width)),
                pl.BlockSpec((1, block, kv), lambda b, *_: (0, b, 0)),
                pl.BlockSpec((1, block, kv), lambda b, *_: (0, b, 0)),
                pl.BlockSpec((1, block), lambda b, *_: (0, b)),
            ],
            out_specs=whole(out.shape),
            scratch_shapes=[
                pltpu.VMEM((groups, KEY_VALUE_HEADS, GROUP * ROWS, HEAD_SIZE), bf16),
                pltpu.VMEM(state, f32),
                pltpu.VMEM(state, f32),
                pltpu.VMEM(state, f32),
            ],
        ),
        compiler_params=params(),
        name="attend",
    )(owners.reshape(-1), queries, keys, values, owners)


def merge_kernel(part_ref, q_ref, kv_ref, out_ref):
    parts, rows, _ = part_ref.shape
    width = QUERY_HEADS * HEAD_SIZE
    kv = KEY_VALUE_HEADS * HEAD_SIZE
    source = lax.broadcasted_iota(jnp.int32, (128, 256), 0)
    target = lax.broadcasted_iota(jnp.int32, (128, 256), 1)
    wanted = (target % 128) * 6 + (target // 128) * 3
    pick = jnp.where(
        (source >= wanted) & (source < wanted + 3) & (target % 128 < QUERY_HEADS), 1.0, 0.0
    ).astype(bf16)
    lane = lax.broadcasted_iota(jnp.int32, (rows, 128), 1)
    own = jnp.zeros((rows, 128), f32)
    for h in range(QUERY_HEADS):
        c = h // GROUP
        product = q_ref[:, h * HEAD_SIZE : (h + 1) * HEAD_SIZE].astype(f32) * kv_ref[
            :, c * HEAD_SIZE : (c + 1) * HEAD_SIZE
        ].astype(f32)
        own = jnp.where(lane == h, jnp.sum(product, axis=1, keepdims=True) * SCALING, own)
    maxima, sums = [], []
    peak = own
    for j in range(parts):
        both = jnp.dot(part_ref[j, :, width:], pick, preferred_element_type=f32)
        maxima.append(both[:, :128])
        sums.append(both[:, 128:])
        peak = jnp.maximum(peak, both[:, :128])
    own_prob = jnp.exp(own - peak).astype(bf16).astype(f32)
    weights = [l * jnp.exp(m - peak) for m, l in zip(maxima, sums)]
    den = own_prob
    for w in weights:
        den = den + w
    own_prob = own_prob / den
    weights = [w / den for w in weights]
    for h in range(QUERY_HEADS):
        c = h // GROUP
        lanes = slice(h * HEAD_SIZE, (h + 1) * HEAD_SIZE)
        acc = own_prob[:, h : h + 1] * kv_ref[
            :, kv + c * HEAD_SIZE : kv + (c + 1) * HEAD_SIZE
        ].astype(f32)
        for j in range(parts):
            acc = acc + weights[j][:, h : h + 1] * part_ref[j, :, lanes].astype(f32)
        out_ref[:, lanes] = acc.astype(bf16)


def merge(part, queries, token_key_value):
    return pl.pallas_call(
        merge_kernel,
        out_shape=jax.ShapeDtypeStruct(queries.shape, bf16),
        compiler_params=params(),
        name="merge",
    )(part, queries, token_key_value)


def routing(expert_ids, mixing, num_gx, group_index):
    local = E // num_gx
    hit = expert_ids[:, :, None] == lax.iota(jnp.int32, E)
    named = jnp.any(hit, axis=1)
    counts = jnp.sum(named.astype(jnp.int32), axis=0).reshape(num_gx, local)
    padded = (counts + ALIGN - 1) // ALIGN * ALIGN
    needed = jnp.max(jnp.sum(padded, axis=1))
    earlier = lax.iota(jnp.int32, local)[:, None] < lax.iota(jnp.int32, local)[None, :]
    starts = jnp.sum(jnp.where(earlier[None], padded[:, :, None], 0), axis=1)
    mine = group_index * local + lax.iota(jnp.int32, local)
    hit_mine = expert_ids[:, :, None] == mine
    mine_named = jnp.any(hit_mine, axis=1)
    weight = jnp.sum(jnp.where(hit_mine, mixing[:, :, None], 0.0), axis=1)
    requests = expert_ids.shape[0]
    before = (lax.iota(jnp.int32, requests)[None, :] < lax.iota(jnp.int32, requests)[:, None])
    rank = jnp.dot(
        before.astype(bf16), mine_named.astype(bf16), preferred_element_type=f32
    ).astype(jnp.int32)
    rank = jnp.where(mine_named, rank, -1)
    start = lax.dynamic_index_in_dim(starts, group_index, 0, False)
    return rank, weight, start, needed


def dispatch_kernel(h_ref, gain_ref, rank_ref, x_ref, square_ref):
    slots = x_ref.shape[1]
    h = h_ref[...].astype(f32)
    square_ref[...] = lax.dot_general(
        jnp.ones((8, h.shape[1]), f32),
        h * h,
        (((1,), (1,)), ((), ())),
        precision=lax.Precision.HIGHEST,
        preferred_element_type=f32,
    )
    scaled = (h * gain_ref[...].astype(f32)).astype(bf16)
    slot = lax.broadcasted_iota(jnp.int32, (slots, h.shape[0]), 0)
    for e in range(x_ref.shape[0]):
        pick = (rank_ref[e : e + 1, :] == slot).astype(f32).astype(bf16)
        x_ref[e] = jnp.dot(pick, scaled, preferred_element_type=f32).astype(bf16)


def dispatch(hidden_all, gain, rank_t, slots):
    requests, features = hidden_all.shape
    return pl.pallas_call(
        dispatch_kernel,
        out_shape=(
            jax.ShapeDtypeStruct((rank_t.shape[0], slots, features), bf16),
            jax.ShapeDtypeStruct((8, requests), f32),
        ),
        compiler_params=params(),
        name="dispatch",
    )(hidden_all, gain.reshape(1, -1), rank_t)


def gate_up_kernel(bit, me_s, start_s, x_ref, gate_ref, up_ref, keep_ref, send_ref, scr):
    step = pl.program_id(0)
    experts = gate_ref.shape[0]
    slots = x_ref.shape[1]
    units = gate_ref.shape[2]
    for i in range(experts):
        e = step * experts + i
        rows = pl.ds(pl.multiple_of(start_s[e], ALIGN), slots)
        x = x_ref[e]
        scr[rows, :units] = jnp.dot(x, gate_ref[i], preferred_element_type=f32).astype(bf16)
        scr[rows, units:] = jnp.dot(x, up_ref[i], preferred_element_type=f32).astype(bf16)

    @pl.when(step == pl.num_programs(0) - 1)
    def _():
        half, rows_each, _ = keep_ref.shape
        me = me_s[0]
        for i in range(half):
            low = i % bit
            other = (i // bit) * 2 * bit + low
            at = jnp.bitwise_xor(me, other) * rows_each
            keep_ref[i] = scr[pl.ds(pl.multiple_of(at, ALIGN), rows_each), :]
            at = jnp.bitwise_xor(me, other + bit) * rows_each
            send_ref[i] = scr[pl.ds(pl.multiple_of(at, ALIGN), rows_each), :]


def gate_up(x, w_gate_up, start, me, capacity, parts, chunk, bit):
    experts, slots, features = x.shape
    units = w_gate_up.shape[2] // (2 * CHUNKS)
    per = min(EXPERTS_PER_STEP, experts)
    out = jax.ShapeDtypeStruct((parts // 2, capacity // parts, 2 * units), bf16)
    return pl.pallas_call(
        functools.partial(gate_up_kernel, bit),
        out_shape=(out, out),
        grid_spec=pltpu.PrefetchScalarGridSpec(
            num_scalar_prefetch=2,
            grid=(experts // per,),
            in_specs=[
                whole(x.shape),
                pl.BlockSpec((per, features, units), lambda s, *_: (s, 0, chunk)),
                pl.BlockSpec((per, features, units), lambda s, *_: (s, 0, CHUNKS + chunk)),
            ],
            out_specs=(whole(out.shape), whole(out.shape)),
            scratch_shapes=[pltpu.VMEM((capacity + slots, 2 * units), bf16)],
        ),
        compiler_params=params(),
        cost_estimate=pl.CostEstimate(
            flops=4 * experts * slots * features * units,
            bytes_accessed=experts * features * units * 4 + out.size * 4,
            transcendentals=0,
        ),
        name="gate_up",
    )(me, start, x, w_gate_up, w_gate_up)


def exchange(x, k, parts):
    return lax.ppermute(x, "gy", [(i, i ^ k) for i in range(parts)])


def scatter_sums(keep, send, order, parts):
    names = [k for k in range(parts) if not k & order[0]]
    total = keep.astype(f32) + exchange(send, order[0], parts).astype(f32)
    for k in order[1:]:
        kept = [i for i, n in enumerate(names) if not n & k]
        sent = [i for i, n in enumerate(names) if n & k]
        rest = jnp.stack([total[i] for i in sent]).astype(bf16)
        total = jnp.stack([total[i] for i in kept]) + exchange(rest, k, parts).astype(f32)
        names = [names[i] for i in kept]
    return total[0]


def gather_rows(x, order, parts):
    names = [0]
    x = x[None]
    for k in order[:-1]:
        x = jnp.concatenate([x, exchange(x, k, parts)], axis=0)
        names = names + [n ^ k for n in names]
    return x, exchange(x, order[-1], parts), names, [n ^ order[-1] for n in names]


def down_kernel(names, me_s, start_s, *refs):
    acts, (rank_ref, weight_ref, w_ref, out_ref, scr, acc) = refs[: len(names)], refs[len(names) :]
    step = pl.program_id(0)
    experts = w_ref.shape[0]
    total, slots = rank_ref.shape[0], scr.shape[0] - acts[0].shape[1] * acts[0].shape[0] * 2
    capacity = scr.shape[0] - slots
    me = me_s[0]

    @pl.when(step == 0)
    def _():
        acc[...] = jnp.zeros(acc.shape, f32)
        scr[capacity:, :] = jnp.zeros((slots, scr.shape[1]), bf16)
        for a, (ref, ns) in enumerate(zip(acts, names)):
            units = ref.shape[2]
            lanes = slice((a // 2) * units, (a // 2 + 1) * units)
            for i, n in enumerate(ns):
                at = jnp.bitwise_xor(me, n) * ref.shape[1]
                scr[pl.ds(pl.multiple_of(at, ALIGN), ref.shape[1]), lanes] = ref[i]

    column = lax.broadcasted_iota(jnp.int32, (total, 128), 1)
    slot = lax.broadcasted_iota(jnp.int32, (total, slots), 1)
    for i in range(experts):
        e = step * experts + i
        rows = pl.ds(pl.multiple_of(start_s[e], ALIGN), slots)
        y = jnp.dot(scr[rows, :], w_ref[i], preferred_element_type=f32).astype(bf16)
        rank = jnp.sum(jnp.where(column == e, rank_ref[...], 0), axis=1, keepdims=True)
        weight = jnp.sum(jnp.where(column == e, weight_ref[...], 0.0), axis=1, keepdims=True)
        pick = (rank == slot).astype(f32).astype(bf16)
        acc[...] += weight * jnp.dot(pick, y, preferred_element_type=f32)

    @pl.when(step == pl.num_programs(0) - 1)
    def _():
        out_ref[...] = acc[...]


def down(acts, names, w_down, start, me, rank, weight, slots):
    experts, hidden_units, features = w_down.shape
    capacity = acts[0].shape[0] * acts[0].shape[1] * 2
    per = min(EXPERTS_PER_STEP, experts)
    total = rank.shape[0]
    pad = ((0, 0), (0, 128 - experts))
    rank = jnp.pad(rank, pad)
    weight = jnp.pad(weight, pad)
    return pl.pallas_call(
        functools.partial(down_kernel, names),
        out_shape=jax.ShapeDtypeStruct((total, features), f32),
        grid_spec=pltpu.PrefetchScalarGridSpec(
            num_scalar_prefetch=2,
            grid=(experts // per,),
            in_specs=[whole(a.shape) for a in acts]
            + [
                whole(rank.shape),
                whole(weight.shape),
                pl.BlockSpec((per, hidden_units, features), lambda s, *_: (s, 0, 0)),
            ],
            out_specs=whole((total, features)),
            scratch_shapes=[
                pltpu.VMEM((capacity + slots, hidden_units), bf16),
                pltpu.VMEM((total, features), f32),
            ],
        ),
        compiler_params=params(),
        name="down",
    )(me, start, *acts, rank, weight, w_down)


def experts_part(capacity, x, square, w_gate_up, w_down, start, rank, weight, me, parts, slots):
    units = w_down.shape[1] // CHUNKS
    rows = capacity // parts
    inv = lax.rsqrt(lax.psum(square, "gy") / D + EPSILON)
    place = jnp.where(rank >= 0, rank + start[None, :], -1)
    here = me[0] * rows + lax.iota(jnp.int32, rows)
    mine = jnp.any(place[None] == here[:, None, None], axis=2)
    scale = jnp.sum(jnp.where(mine, inv[None, :], 0.0), axis=1)[:, None]
    bits = [1 << i for i in range(parts.bit_length() - 1)]
    acts, names = [], []
    for chunk in range(CHUNKS):
        order = bits if chunk % 2 == 0 else bits[1:] + bits[:1]
        keep, send = gate_up(x, w_gate_up, start, me, capacity, parts, chunk, order[0])
        both = scatter_sums(keep, send, order, parts)
        gate = both[:, :units] * scale
        up = both[:, units:] * scale
        act = (jax.nn.silu(gate) * up).astype(bf16)
        left, right, left_names, right_names = gather_rows(act, order[::-1], parts)
        acts += [left, right]
        names += [left_names, right_names]
    return down(acts, names, w_down, start, me, rank, weight, slots)


def out_kernel(a_ref, w_ref, r_ref, o_ref):
    a = a_ref[...]
    o_ref[...] = (
        r_ref[...].astype(f32) + jnp.dot(a, w_ref[...], preferred_element_type=f32)
    ).astype(bf16)


def project(attention, out_weight, residual):
    return pl.pallas_call(
        out_kernel,
        out_shape=jax.ShapeDtypeStruct(residual.shape, bf16),
        compiler_params=params(),
        name="project",
    )(attention, out_weight, residual)


def shards(
    queries,
    token_key_value,
    group_cached_keys,
    group_cached_values,
    owners,
    out_weight,
    residual,
    norm_gain,
    expert_ids,
    gate_logits,
    w_gate_up,
    w_down,
):
    rows, width = queries.shape
    parts = lax.axis_size("gy")
    num_gx = lax.axis_size("gx")
    me_y = lax.axis_index("gy")
    me_x = lax.axis_index("gx")
    me = jnp.full((1,), me_y, jnp.int32)
    each = rows // parts
    slots = num_gx * CAPS
    local = w_gate_up.shape[0]

    part = attend_local(queries, group_cached_keys, group_cached_values, owners, parts)
    part = lax.all_to_all(part, "gy", 0, 0)
    attention = merge(
        part,
        lax.dynamic_slice_in_dim(queries, me_y * each, each, 0),
        lax.dynamic_slice_in_dim(token_key_value, me_y * each, each, 0),
    )
    attention = lax.all_to_all(
        jnp.broadcast_to(attention[None], (parts,) + attention.shape), "gy", 0, 0
    ).reshape(rows, width)
    hidden = project(attention, out_weight, residual)
    hidden_all = lax.all_gather(hidden, "gx", axis=0, tiled=True)

    mixing = jax.nn.softmax(gate_logits, axis=-1)
    rank, weight, start, needed = routing(expert_ids, mixing, num_gx, me_x)
    x, square = dispatch(hidden_all, norm_gain, rank.T, slots)

    capacity = local * (-(-slots // ALIGN) * ALIGN)
    sizes = [c for c in (512, 640) if c < capacity and c % (ALIGN * parts) == 0] + [capacity]
    branch = sum((needed > c).astype(jnp.int32) for c in sizes[:-1])
    operands = (x, square[0], w_gate_up, w_down, start, rank, weight, me)
    routed = lax.switch(
        branch,
        [
            lambda *o, c=c: experts_part(c, *o, parts=parts, slots=slots)
            for c in sizes
        ],
        *operands,
    )
    routed = lax.all_to_all(routed.reshape(num_gx, rows, -1), "gx", 0, 0)
    return hidden.astype(f32) + jnp.sum(routed, axis=0)


def solution(mesh):
    placed = (
        P("gx", None),
        P("gx", None),
        P("gx", "gy", None),
        P("gx", "gy", None),
        P("gx", "gy"),
        P(None, "gy"),
        P("gx", "gy"),
        P("gy"),
        P(),
        P(),
        P("gx", "gy", None),
        P("gx", None, "gy"),
    )
    return jax.shard_map(
        shards, mesh=mesh, in_specs=placed, out_specs=P("gx", "gy"), check_vma=False
    )
```

```python
import functools

import jax
import jax.numpy as jnp
from jax import lax
from jax.experimental import pallas as pl
from jax.experimental.pallas import tpu as pltpu
from jax.sharding import PartitionSpec as P

D = 2560
QUERY_HEADS = 20
KEY_VALUE_HEADS = 4
HEAD_SIZE = 128
GROUP = QUERY_HEADS // KEY_VALUE_HEADS
E = 64
TOPK = 6
CAPS = 12

LOWEST = -1e30
EPSILON = 1e-05
SCALING = HEAD_SIZE ** (-0.5)
BLOCK = 512
ROWS = 16
ALIGN = 8
CHUNKS = 4
UNROLL = 4

f32 = jnp.float32
bf16 = jnp.bfloat16
VMEM_LIMIT = 56 * 1024 * 1024


def params(**more):
    return pltpu.CompilerParams(vmem_limit_bytes=VMEM_LIMIT, **more)


def whole(shape):
    return pl.BlockSpec(shape, lambda *_: (0,) * len(shape))


def attend_kernel(
    owner_s, q_ref, own_ref, k_hbm, v_hbm, out_ref, k_scr, v_scr, q_scr, m_scr, l_scr, acc_scr, sem
):
    groups = q_scr.shape[0]
    blocks = sem.shape[1]
    block = k_scr.shape[0] // blocks

    def copies(b):
        rows = pl.ds(b * block, block)
        return (
            pltpu.make_async_copy(k_hbm.at[0, rows], k_scr.at[rows], sem.at[0, b]),
            pltpu.make_async_copy(v_hbm.at[0, rows], v_scr.at[rows], sem.at[1, b]),
        )

    for b in range(blocks):
        for copy in copies(b):
            copy.start()
    for rg in range(groups):
        for c in range(KEY_VALUE_HEADS):
            for g in range(GROUP):
                h = c * GROUP + g
                q_scr[rg, c, g * ROWS : (g + 1) * ROWS, :] = q_ref[
                    rg * ROWS : (rg + 1) * ROWS, h * HEAD_SIZE : (h + 1) * HEAD_SIZE
                ]
    m_scr[...] = jnp.full(m_scr.shape, LOWEST, f32)
    l_scr[...] = jnp.zeros(l_scr.shape, f32)
    acc_scr[...] = jnp.zeros(acc_scr.shape, f32)
    heads = range(KEY_VALUE_HEADS)
    lanes = [slice(c * HEAD_SIZE, (c + 1) * HEAD_SIZE) for c in heads]

    def walk(b, carry):
        for copy in copies(b):
            copy.wait()
        at = pl.multiple_of(b * block, block)
        rows = pl.ds(at, block)
        owner = own_ref[0:1, rows]

        def visit(rg, carry):
            ids = rg * ROWS + lax.broadcasted_iota(jnp.int32, (ROWS, block), 0)
            member = owner == ids
            states = [(m_scr[rg, c], l_scr[rg, c], acc_scr[rg, c]) for c in heads]
            scores = [
                lax.dot_general(
                    q_scr[rg, c],
                    k_scr[rows, lanes[c]],
                    (((1,), (1,)), ((), ())),
                    preferred_element_type=f32,
                )
                * SCALING
                for c in heads
            ]
            results = []
            for c in heads:
                s = jnp.where(member[None], scores[c].reshape(GROUP, ROWS, block), LOWEST)
                s = s.reshape(GROUP * ROWS, block)
                m_old, l_old, acc_old = states[c]
                m_new = jnp.maximum(m_old, jnp.max(s, axis=1, keepdims=True))
                alpha = jnp.exp(m_old - m_new)
                p = jnp.exp(s - m_new[:, :1]).astype(bf16)
                l_new = l_old * alpha + jnp.sum(p.astype(f32), axis=1, keepdims=True)
                acc_new = acc_old * alpha + jnp.dot(
                    p, v_scr[rows, lanes[c]], preferred_element_type=f32
                )
                results.append((m_new, l_new, acc_new))
            for c in heads:
                m_scr[rg, c], l_scr[rg, c], acc_scr[rg, c] = results[c]
            return carry

        first = owner_s[at] // ROWS
        last = owner_s[at + block - 1] // ROWS
        return lax.fori_loop(first, last + 1, visit, carry)

    lax.fori_loop(0, blocks, walk, 0)

    width = QUERY_HEADS * HEAD_SIZE
    lane = lax.broadcasted_iota(jnp.int32, (ROWS, 128), 1)
    piece = lane % 3
    per = out_ref.shape[1]
    for rg in range(groups):

        def put(value, lanes):
            if per >= ROWS:
                at = rg * ROWS
                out_ref[at // per, at % per : at % per + ROWS, lanes] = value.astype(bf16)
            else:
                for i in range(ROWS // per):
                    out_ref[(rg * ROWS) // per + i, :, lanes] = value[
                        i * per : (i + 1) * per
                    ].astype(bf16)

        tail = jnp.zeros((ROWS, 128), f32)
        for c in heads:
            for g in range(GROUP):
                h = c * GROUP + g
                rows = slice(g * ROWS, (g + 1) * ROWS)
                m = m_scr[rg, c, rows, :]
                l = l_scr[rg, c, rows, :]
                tail = jnp.where(lane // 6 == h, jnp.where(lane % 6 < 3, m, l), tail)
                put(
                    acc_scr[rg, c, rows, :] / jnp.maximum(l, 1e-30),
                    slice(h * HEAD_SIZE, (h + 1) * HEAD_SIZE),
                )
        high = tail.astype(bf16).astype(f32)
        rest = tail - high
        middle = rest.astype(bf16).astype(f32)
        low = (rest - middle).astype(bf16).astype(f32)
        put(
            jnp.where(piece == 0, high, jnp.where(piece == 1, middle, low)),
            slice(width, width + 128),
        )


def attend_local(queries, keys, values, owners, parts):
    rows, width = queries.shape
    positions, kv = keys.shape[1:]
    block = min(BLOCK, positions)
    groups = rows // ROWS
    state = (groups, KEY_VALUE_HEADS, GROUP * ROWS, 128)
    out = jax.ShapeDtypeStruct((parts, rows // parts, width + 128), bf16)
    return pl.pallas_call(
        attend_kernel,
        out_shape=out,
        grid_spec=pltpu.PrefetchScalarGridSpec(
            num_scalar_prefetch=1,
            grid=(1,),
            in_specs=[
                whole((rows, width)),
                whole((1, positions)),
                pl.BlockSpec(memory_space=pl.ANY),
                pl.BlockSpec(memory_space=pl.ANY),
            ],
            out_specs=whole(out.shape),
            scratch_shapes=[
                pltpu.VMEM((positions, kv), bf16),
                pltpu.VMEM((positions, kv), bf16),
                pltpu.VMEM((groups, KEY_VALUE_HEADS, GROUP * ROWS, HEAD_SIZE), bf16),
                pltpu.VMEM(state, f32),
                pltpu.VMEM(state, f32),
                pltpu.VMEM(state, f32),
                pltpu.SemaphoreType.DMA((2, positions // block)),
            ],
        ),
        compiler_params=params(),
        name="attend",
    )(owners.reshape(-1), queries, owners, keys, values)


def merge_kernel(part_ref, q_ref, kv_ref, out_ref):
    parts, rows, _ = part_ref.shape
    width = QUERY_HEADS * HEAD_SIZE
    kv = KEY_VALUE_HEADS * HEAD_SIZE
    source = lax.broadcasted_iota(jnp.int32, (128, 256), 0)
    target = lax.broadcasted_iota(jnp.int32, (128, 256), 1)
    wanted = (target % 128) * 6 + (target // 128) * 3
    pick = jnp.where(
        (source >= wanted) & (source < wanted + 3) & (target % 128 < QUERY_HEADS), 1.0, 0.0
    ).astype(bf16)
    lane = lax.broadcasted_iota(jnp.int32, (rows, 128), 1)
    own = jnp.zeros((rows, 128), f32)
    for h in range(QUERY_HEADS):
        c = h // GROUP
        product = q_ref[:, h * HEAD_SIZE : (h + 1) * HEAD_SIZE].astype(f32) * kv_ref[
            :, c * HEAD_SIZE : (c + 1) * HEAD_SIZE
        ].astype(f32)
        own = jnp.where(lane == h, jnp.sum(product, axis=1, keepdims=True) * SCALING, own)
    maxima, sums = [], []
    peak = own
    for j in range(parts):
        both = jnp.dot(part_ref[j, :, width:], pick, preferred_element_type=f32)
        maxima.append(both[:, :128])
        sums.append(both[:, 128:])
        peak = jnp.maximum(peak, both[:, :128])
    own_prob = jnp.exp(own - peak).astype(bf16).astype(f32)
    weights = [l * jnp.exp(m - peak) for m, l in zip(maxima, sums)]
    den = own_prob
    for w in weights:
        den = den + w
    own_prob = own_prob / den
    weights = [w / den for w in weights]
    for h in range(QUERY_HEADS):
        c = h // GROUP
        lanes = slice(h * HEAD_SIZE, (h + 1) * HEAD_SIZE)
        acc = own_prob[:, h : h + 1] * kv_ref[
            :, kv + c * HEAD_SIZE : kv + (c + 1) * HEAD_SIZE
        ].astype(f32)
        for j in range(parts):
            acc = acc + weights[j][:, h : h + 1] * part_ref[j, :, lanes].astype(f32)
        out_ref[:, lanes] = acc.astype(bf16)


def merge(part, queries, token_key_value):
    return pl.pallas_call(
        merge_kernel,
        out_shape=jax.ShapeDtypeStruct(queries.shape, bf16),
        compiler_params=params(),
        name="merge",
    )(part, queries, token_key_value)


def routing(expert_ids, mixing, num_gx, group_index):
    local = E // num_gx
    hit = expert_ids[:, :, None] == lax.iota(jnp.int32, E)
    named = jnp.any(hit, axis=1)
    counts = jnp.sum(named.astype(jnp.int32), axis=0).reshape(num_gx, local)
    needed = jnp.max(jnp.sum(counts, axis=1))
    earlier = lax.iota(jnp.int32, local)[:, None] < lax.iota(jnp.int32, local)[None, :]
    starts = jnp.sum(jnp.where(earlier[None], counts[:, :, None], 0), axis=1)
    mine = group_index * local + lax.iota(jnp.int32, local)
    hit_mine = expert_ids[:, :, None] == mine
    mine_named = jnp.any(hit_mine, axis=1)
    weight = jnp.sum(jnp.where(hit_mine, mixing[:, :, None], 0.0), axis=1)
    requests = expert_ids.shape[0]
    before = (lax.iota(jnp.int32, requests)[None, :] < lax.iota(jnp.int32, requests)[:, None])
    rank = jnp.dot(
        before.astype(bf16), mine_named.astype(bf16), preferred_element_type=f32
    ).astype(jnp.int32)
    start = lax.dynamic_index_in_dim(starts, group_index, 0, False)
    place = jnp.where(mine_named, rank + start[None, :], -1)
    base = start // ALIGN * ALIGN
    rank = jnp.where(mine_named, place - base[None, :], -1)
    return rank, place, weight, base, needed


def dispatch_kernel(h_ref, gain_ref, rank_ref, x_ref, square_ref):
    slots = x_ref.shape[1]
    h = h_ref[...].astype(f32)
    square_ref[...] = lax.dot_general(
        jnp.ones((8, h.shape[1]), f32),
        h * h,
        (((1,), (1,)), ((), ())),
        precision=lax.Precision.HIGHEST,
        preferred_element_type=f32,
    )
    scaled = (h * gain_ref[...].astype(f32)).astype(bf16)
    slot = lax.broadcasted_iota(jnp.int32, (slots, h.shape[0]), 0)
    for e in range(x_ref.shape[0]):
        pick = (rank_ref[e : e + 1, :] == slot).astype(f32).astype(bf16)
        x_ref[e] = jnp.dot(pick, scaled, preferred_element_type=f32).astype(bf16)


def dispatch(hidden_all, gain, rank_t, slots):
    requests, features = hidden_all.shape
    return pl.pallas_call(
        dispatch_kernel,
        out_shape=(
            jax.ShapeDtypeStruct((rank_t.shape[0], slots, features), bf16),
            jax.ShapeDtypeStruct((8, requests), f32),
        ),
        compiler_params=params(),
        name="dispatch",
    )(hidden_all, gain.reshape(1, -1), rank_t)


def gate_up_kernel(bit, chunk, me_s, base_s, x_ref, w_hbm, keep_ref, send_ref, scr, buf, sem):
    experts, slots, _ = x_ref.shape
    units = buf.shape[3]
    hidden_units = units * CHUNKS

    def copies(e):
        return [
            pltpu.make_async_copy(
                w_hbm.at[e, :, pl.ds(half * hidden_units + chunk * units, units)],
                buf.at[e, half],
                sem.at[e, half],
            )
            for half in range(2)
        ]

    for e in range(experts):
        for copy in copies(e):
            copy.start()
    scr[...] = jnp.zeros(scr.shape, f32)
    unroll = min(UNROLL, experts)

    def visit(step, carry):
        for i in range(unroll):
            e = step * unroll + i
            rows = pl.ds(pl.multiple_of(base_s[e], ALIGN), slots)
            x = x_ref[e]
            for half, copy in enumerate(copies(e)):
                copy.wait()
                lanes = slice(half * units, (half + 1) * units)
                scr[rows, lanes] += jnp.dot(x, buf[e, half], preferred_element_type=f32)
        return carry

    lax.fori_loop(0, experts // unroll, visit, 0)
    half, each, _ = keep_ref.shape
    me = me_s[0]
    for i in range(half):
        other = (i // bit) * 2 * bit + i % bit
        at = jnp.bitwise_xor(me, other) * each
        keep_ref[i] = scr[pl.ds(pl.multiple_of(at, ALIGN), each), :].astype(bf16)
        at = jnp.bitwise_xor(me, other + bit) * each
        send_ref[i] = scr[pl.ds(pl.multiple_of(at, ALIGN), each), :].astype(bf16)


def gate_up(x, w_gate_up, base, me, capacity, parts, chunk, bit):
    experts, slots, features = x.shape
    units = w_gate_up.shape[2] // (2 * CHUNKS)
    out = jax.ShapeDtypeStruct((parts // 2, capacity // parts, 2 * units), bf16)
    return pl.pallas_call(
        functools.partial(gate_up_kernel, bit, chunk),
        out_shape=(out, out),
        grid_spec=pltpu.PrefetchScalarGridSpec(
            num_scalar_prefetch=2,
            grid=(1,),
            in_specs=[whole(x.shape), pl.BlockSpec(memory_space=pl.ANY)],
            out_specs=(whole(out.shape), whole(out.shape)),
            scratch_shapes=[
                pltpu.VMEM((capacity + slots, 2 * units), f32),
                pltpu.VMEM((experts, 2, features, units), bf16),
                pltpu.SemaphoreType.DMA((experts, 2)),
            ],
        ),
        compiler_params=params(),
        cost_estimate=pl.CostEstimate(
            flops=4 * experts * slots * features * units,
            bytes_accessed=experts * features * units * 4 + out.size * 4,
            transcendentals=0,
        ),
        name="gate_up",
    )(me, base, x, w_gate_up)


def exchange(x, k, parts):
    return lax.ppermute(x, "gy", [(i, i ^ k) for i in range(parts)])


def scatter_sums(keep, send, order, parts):
    names = [k for k in range(parts) if not k & order[0]]
    total = keep.astype(f32) + exchange(send, order[0], parts).astype(f32)
    for k in order[1:]:
        kept = [i for i, n in enumerate(names) if not n & k]
        sent = [i for i, n in enumerate(names) if n & k]
        rest = jnp.stack([total[i] for i in sent]).astype(bf16)
        total = jnp.stack([total[i] for i in kept]) + exchange(rest, k, parts).astype(f32)
        names = [names[i] for i in kept]
    return total[0]


def gather_rows(x, order, parts):
    names = [0]
    x = x[None]
    for k in order[:-1]:
        x = jnp.concatenate([x, exchange(x, k, parts)], axis=0)
        names = names + [n ^ k for n in names]
    return x, exchange(x, order[-1], parts), names, [n ^ order[-1] for n in names]


def down_kernel(names, me_s, base_s, *refs):
    acts = refs[: len(names)]
    rank_ref, weight_ref, w_hbm, out_ref, scr, buf, sem = refs[len(names) :]
    experts = buf.shape[0]
    each = acts[0].shape[1]
    capacity = 2 * acts[0].shape[0] * each
    slots = scr.shape[0] - capacity
    total = rank_ref.shape[0]
    me = me_s[0]

    def fetch(e):
        return pltpu.make_async_copy(w_hbm.at[e], buf.at[e], sem.at[e])

    for e in range(experts):
        fetch(e).start()
    scr[capacity:, :] = jnp.zeros((slots, scr.shape[1]), f32)
    for a, (ref, ns) in enumerate(zip(acts, names)):
        units = ref.shape[2]
        lanes = slice((a // 2) * units, (a // 2 + 1) * units)
        for i, n in enumerate(ns):
            at = jnp.bitwise_xor(me, n) * each
            scr[pl.ds(pl.multiple_of(at, ALIGN), each), lanes] = ref[i].astype(f32)
    out_ref[...] = jnp.zeros(out_ref.shape, f32)
    column = lax.broadcasted_iota(jnp.int32, (total, 128), 1)
    slot = lax.broadcasted_iota(jnp.int32, (total, slots), 1)
    unroll = min(UNROLL, experts)

    def visit(step, carry):
        add = None
        for i in range(unroll):
            e = step * unroll + i
            rows = pl.ds(pl.multiple_of(base_s[e], ALIGN), slots)
            x = scr[rows, :].astype(bf16)
            fetch(e).wait()
            y = lax.dot_general(
                x, buf[e], (((1,), (1,)), ((), ())), preferred_element_type=f32
            ).astype(bf16)
            rank = jnp.sum(jnp.where(column == e, rank_ref[...], 0), axis=1, keepdims=True)
            weight = jnp.sum(
                jnp.where(column == e, weight_ref[...], 0.0), axis=1, keepdims=True
            )
            pick = (rank == slot).astype(f32).astype(bf16)
            term = weight * jnp.dot(pick, y, preferred_element_type=f32)
            add = term if add is None else add + term
        out_ref[...] += add
        return carry

    lax.fori_loop(0, experts // unroll, visit, 0)


def down(acts, names, w_down_t, base, me, rank, weight, slots):
    experts, features, hidden_units = w_down_t.shape
    capacity = acts[0].shape[0] * acts[0].shape[1] * 2
    total = rank.shape[0]
    pad = ((0, 0), (0, 128 - experts))
    rank = jnp.pad(rank, pad)
    weight = jnp.pad(weight, pad)
    return pl.pallas_call(
        functools.partial(down_kernel, names),
        out_shape=jax.ShapeDtypeStruct((total, features), f32),
        grid_spec=pltpu.PrefetchScalarGridSpec(
            num_scalar_prefetch=2,
            grid=(1,),
            in_specs=[whole(a.shape) for a in acts]
            + [whole(rank.shape), whole(weight.shape), pl.BlockSpec(memory_space=pl.ANY)],
            out_specs=whole((total, features)),
            scratch_shapes=[
                pltpu.VMEM((capacity + slots, hidden_units), f32),
                pltpu.VMEM(w_down_t.shape, bf16),
                pltpu.SemaphoreType.DMA((experts,)),
            ],
        ),
        compiler_params=params(),
        name="down",
    )(me, base, *acts, rank, weight, w_down_t)


def sum_over_gy(x, parts):
    k = 1
    while k < parts:
        x = x + exchange(x, k, parts)
        k *= 2
    return x


def experts_part(capacity, x, square, w_gate_up, w_down_t, base, rank, place, weight, me, parts, slots):
    units = w_down_t.shape[2] // CHUNKS
    rows = capacity // parts
    here = me[0] * rows + lax.iota(jnp.int32, rows)
    mine = jnp.any(place[None] == here[:, None, None], axis=2)
    bits = [1 << i for i in range(parts.bit_length() - 1)]
    acts, names = [], []
    scale = None
    for chunk in range(CHUNKS):
        order = bits if chunk % 2 == 0 else bits[1:] + bits[:1]
        keep, send = gate_up(x, w_gate_up, base, me, capacity, parts, chunk, order[0])
        both = scatter_sums(keep, send, order, parts)
        if scale is None:
            inv = lax.rsqrt(sum_over_gy(square, parts).reshape(-1) / D + EPSILON)
            scale = jnp.sum(jnp.where(mine, inv[None, :], 0.0), axis=1)[:, None]
        gate = both[:, :units] * scale
        up = both[:, units:] * scale
        act = (jax.nn.silu(gate) * up).astype(bf16)
        left, right, left_names, right_names = gather_rows(act, order[::-1], parts)
        acts += [left, right]
        names += [left_names, right_names]
    return down(acts, names, w_down_t, base, me, rank, weight, slots)


def out_kernel(a_ref, w_ref, r_ref, o_ref):
    projected = lax.dot_general(
        a_ref[...], w_ref[...], (((1,), (1,)), ((), ())), preferred_element_type=f32
    )
    o_ref[...] = (r_ref[...].astype(f32) + projected).astype(bf16)


def project(attention, out_weight, residual):
    return pl.pallas_call(
        out_kernel,
        out_shape=jax.ShapeDtypeStruct(residual.shape, bf16),
        compiler_params=params(),
        name="project",
    )(attention, out_weight, residual)


def shards(
    queries,
    token_key_value,
    group_cached_keys,
    group_cached_values,
    owners,
    out_weight,
    residual,
    norm_gain,
    expert_ids,
    gate_logits,
    w_gate_up,
    w_down,
):
    rows, width = queries.shape
    parts = lax.axis_size("gy")
    num_gx = lax.axis_size("gx")
    me_y = lax.axis_index("gy")
    me_x = lax.axis_index("gx")
    me = jnp.full((1,), me_y, jnp.int32)
    each = rows // parts
    slots = -(-(num_gx * CAPS + ALIGN - 1) // ALIGN) * ALIGN
    local = w_gate_up.shape[0]

    part = attend_local(queries, group_cached_keys, group_cached_values, owners, parts)
    part = lax.all_to_all(part, "gy", 0, 0)
    attention = merge(
        part,
        lax.dynamic_slice_in_dim(queries, me_y * each, each, 0),
        lax.dynamic_slice_in_dim(token_key_value, me_y * each, each, 0),
    )
    attention = lax.all_to_all(
        jnp.broadcast_to(attention[None], (parts,) + attention.shape), "gy", 0, 0
    ).reshape(rows, width)
    hidden = project(attention, out_weight.T, residual)
    hidden_all = lax.all_gather(hidden, "gx", axis=0, tiled=True)

    mixing = jax.nn.softmax(gate_logits, axis=-1)
    rank, place, weight, base, needed = routing(expert_ids, mixing, num_gx, me_x)
    x, square = dispatch(hidden_all, norm_gain, rank.T, slots)

    capacity = local * num_gx * CAPS
    sizes = [c for c in (448, 512) if c < capacity and c % (ALIGN * parts) == 0] + [capacity]
    branch = sum((needed > c).astype(jnp.int32) for c in sizes[:-1])
    operands = (
        x,
        square[0].reshape(-1, 128),
        w_gate_up,
        jnp.swapaxes(w_down, 1, 2),
        base,
        rank,
        place,
        weight,
        me,
    )
    routed = lax.switch(
        branch,
        [lambda *o, c=c: experts_part(c, *o, parts=parts, slots=slots) for c in sizes],
        *operands,
    )
    routed = lax.all_to_all(routed.reshape(num_gx, rows, -1), "gx", 0, 0)
    return hidden.astype(f32) + jnp.sum(routed, axis=0)


def solution(mesh):
    placed = (
        P("gx", None),
        P("gx", None),
        P("gx", "gy", None),
        P("gx", "gy", None),
        P("gx", "gy"),
        P(None, "gy"),
        P("gx", "gy"),
        P("gy"),
        P(),
        P(),
        P("gx", "gy", None),
        P("gx", None, "gy"),
    )
    return jax.shard_map(
        shards, mesh=mesh, in_specs=placed, out_specs=P("gx", "gy"), check_vma=False
    )
```

```python
import functools

import jax
import jax.numpy as jnp
from jax import lax
from jax.experimental import pallas as pl
from jax.experimental.pallas import tpu as pltpu
from jax.sharding import PartitionSpec as P

D = 2560
QUERY_HEADS = 20
KEY_VALUE_HEADS = 4
HEAD_SIZE = 128
GROUP = QUERY_HEADS // KEY_VALUE_HEADS
E = 64
TOPK = 6
CAPS = 12

LOWEST = -1e30
EPSILON = 1e-05
SCALING = HEAD_SIZE ** (-0.5)
BLOCK = 1024
ROWS = 16
ALIGN = 8
CHUNKS = 4
UNROLL = 2

f32 = jnp.float32
bf16 = jnp.bfloat16
MIB = 1024 * 1024


def params(mib):
    return pltpu.CompilerParams(vmem_limit_bytes=mib * MIB)


def whole(shape):
    return pl.BlockSpec(shape, lambda *_: (0,) * len(shape))


def attend_kernel(
    owner_s, q_ref, own_ref, k_hbm, v_hbm, out_ref, k_scr, v_scr, q_scr, m_scr, l_scr, acc_scr, sem
):
    groups = q_scr.shape[0]
    blocks = sem.shape[1]
    block = k_scr.shape[0] // blocks

    def copies(b):
        rows = pl.ds(b * block, block)
        return (
            pltpu.make_async_copy(k_hbm.at[0, rows], k_scr.at[rows], sem.at[0, b]),
            pltpu.make_async_copy(v_hbm.at[0, rows], v_scr.at[rows], sem.at[1, b]),
        )

    for b in range(blocks):
        for copy in copies(b):
            copy.start()
    for rg in range(groups):
        for c in range(KEY_VALUE_HEADS):
            for g in range(GROUP):
                h = c * GROUP + g
                q_scr[rg, c, g * ROWS : (g + 1) * ROWS, :] = q_ref[
                    rg * ROWS : (rg + 1) * ROWS, h * HEAD_SIZE : (h + 1) * HEAD_SIZE
                ]
    m_scr[...] = jnp.full(m_scr.shape, LOWEST, f32)
    l_scr[...] = jnp.zeros(l_scr.shape, f32)
    acc_scr[...] = jnp.zeros(acc_scr.shape, f32)
    heads = range(KEY_VALUE_HEADS)
    lanes = [slice(c * HEAD_SIZE, (c + 1) * HEAD_SIZE) for c in heads]

    def walk(b, carry):
        for copy in copies(b):
            copy.wait()
        at = pl.multiple_of(b * block, block)
        rows = pl.ds(at, block)
        owner = own_ref[0:1, rows]

        def visit(rg, carry):
            ids = rg * ROWS + lax.broadcasted_iota(jnp.int32, (ROWS, block), 0)
            member = owner == ids
            states = [(m_scr[rg, c], l_scr[rg, c], acc_scr[rg, c]) for c in heads]
            scores = [
                lax.dot_general(
                    q_scr[rg, c],
                    k_scr[rows, lanes[c]],
                    (((1,), (1,)), ((), ())),
                    preferred_element_type=f32,
                )
                * SCALING
                for c in heads
            ]
            results = []
            for c in heads:
                s = jnp.where(member[None], scores[c].reshape(GROUP, ROWS, block), LOWEST)
                s = s.reshape(GROUP * ROWS, block)
                m_old, l_old, acc_old = states[c]
                m_new = jnp.maximum(m_old, jnp.max(s, axis=1, keepdims=True))
                alpha = jnp.exp(m_old - m_new)
                p = jnp.exp(s - m_new[:, :1]).astype(bf16)
                l_new = l_old * alpha + jnp.sum(p.astype(f32), axis=1, keepdims=True)
                acc_new = acc_old * alpha + jnp.dot(
                    p, v_scr[rows, lanes[c]], preferred_element_type=f32
                )
                results.append((m_new, l_new, acc_new))
            for c in heads:
                m_scr[rg, c], l_scr[rg, c], acc_scr[rg, c] = results[c]
            return carry

        first = owner_s[at] // ROWS
        last = owner_s[at + block - 1] // ROWS
        return lax.fori_loop(first, last + 1, visit, carry)

    lax.fori_loop(0, blocks, walk, 0)

    width = QUERY_HEADS * HEAD_SIZE
    lane = lax.broadcasted_iota(jnp.int32, (ROWS, 128), 1)
    piece = lane % 3
    per = out_ref.shape[1]
    for rg in range(groups):

        def put(value, lanes):
            if per >= ROWS:
                at = rg * ROWS
                out_ref[at // per, at % per : at % per + ROWS, lanes] = value.astype(bf16)
            else:
                for i in range(ROWS // per):
                    out_ref[(rg * ROWS) // per + i, :, lanes] = value[
                        i * per : (i + 1) * per
                    ].astype(bf16)

        tail = jnp.zeros((ROWS, 128), f32)
        for c in heads:
            for g in range(GROUP):
                h = c * GROUP + g
                rows = slice(g * ROWS, (g + 1) * ROWS)
                m = m_scr[rg, c, rows, :]
                l = l_scr[rg, c, rows, :]
                tail = jnp.where(lane // 6 == h, jnp.where(lane % 6 < 3, m, l), tail)
                put(
                    acc_scr[rg, c, rows, :] / jnp.maximum(l, 1e-30),
                    slice(h * HEAD_SIZE, (h + 1) * HEAD_SIZE),
                )
        high = tail.astype(bf16).astype(f32)
        rest = tail - high
        middle = rest.astype(bf16).astype(f32)
        low = (rest - middle).astype(bf16).astype(f32)
        put(
            jnp.where(piece == 0, high, jnp.where(piece == 1, middle, low)),
            slice(width, width + 128),
        )


def attend_local(queries, keys, values, owners, parts):
    rows, width = queries.shape
    positions, kv = keys.shape[1:]
    block = min(BLOCK, positions)
    groups = rows // ROWS
    state = (groups, KEY_VALUE_HEADS, GROUP * ROWS, 128)
    out = jax.ShapeDtypeStruct((parts, rows // parts, width + 128), bf16)
    return pl.pallas_call(
        attend_kernel,
        out_shape=out,
        grid_spec=pltpu.PrefetchScalarGridSpec(
            num_scalar_prefetch=1,
            grid=(1,),
            in_specs=[
                whole((rows, width)),
                whole((1, positions)),
                pl.BlockSpec(memory_space=pltpu.HBM),
                pl.BlockSpec(memory_space=pltpu.HBM),
            ],
            out_specs=whole(out.shape),
            scratch_shapes=[
                pltpu.VMEM((positions, kv), bf16),
                pltpu.VMEM((positions, kv), bf16),
                pltpu.VMEM((groups, KEY_VALUE_HEADS, GROUP * ROWS, HEAD_SIZE), bf16),
                pltpu.VMEM(state, f32),
                pltpu.VMEM(state, f32),
                pltpu.VMEM(state, f32),
                pltpu.SemaphoreType.DMA((2, positions // block)),
            ],
        ),
        compiler_params=params(56),
        name="attend",
    )(owners.reshape(-1), queries, owners, keys, values)


def merge_kernel(part_ref, q_ref, kv_ref, out_ref):
    parts, rows, _ = part_ref.shape
    width = QUERY_HEADS * HEAD_SIZE
    kv = KEY_VALUE_HEADS * HEAD_SIZE
    source = lax.broadcasted_iota(jnp.int32, (128, 256), 0)
    target = lax.broadcasted_iota(jnp.int32, (128, 256), 1)
    wanted = (target % 128) * 6 + (target // 128) * 3
    pick = jnp.where(
        (source >= wanted) & (source < wanted + 3) & (target % 128 < QUERY_HEADS), 1.0, 0.0
    ).astype(bf16)
    lane = lax.broadcasted_iota(jnp.int32, (rows, 128), 1)
    own = jnp.zeros((rows, 128), f32)
    for h in range(QUERY_HEADS):
        c = h // GROUP
        product = q_ref[:, h * HEAD_SIZE : (h + 1) * HEAD_SIZE].astype(f32) * kv_ref[
            :, c * HEAD_SIZE : (c + 1) * HEAD_SIZE
        ].astype(f32)
        own = jnp.where(lane == h, jnp.sum(product, axis=1, keepdims=True) * SCALING, own)
    maxima, sums = [], []
    peak = own
    for j in range(parts):
        both = jnp.dot(part_ref[j, :, width:], pick, preferred_element_type=f32)
        maxima.append(both[:, :128])
        sums.append(both[:, 128:])
        peak = jnp.maximum(peak, both[:, :128])
    own_prob = jnp.exp(own - peak).astype(bf16).astype(f32)
    weights = [l * jnp.exp(m - peak) for m, l in zip(maxima, sums)]
    den = own_prob
    for w in weights:
        den = den + w
    own_prob = own_prob / den
    weights = [w / den for w in weights]
    for h in range(QUERY_HEADS):
        c = h // GROUP
        lanes = slice(h * HEAD_SIZE, (h + 1) * HEAD_SIZE)
        acc = own_prob[:, h : h + 1] * kv_ref[
            :, kv + c * HEAD_SIZE : kv + (c + 1) * HEAD_SIZE
        ].astype(f32)
        for j in range(parts):
            acc = acc + weights[j][:, h : h + 1] * part_ref[j, :, lanes].astype(f32)
        out_ref[:, lanes] = acc.astype(bf16)


def merge(part, queries, token_key_value):
    return pl.pallas_call(
        merge_kernel,
        out_shape=jax.ShapeDtypeStruct(queries.shape, bf16),
        compiler_params=params(6),
        name="merge",
    )(part, queries, token_key_value)


def routing(expert_ids, mixing, num_gx, group_index):
    local = E // num_gx
    hit = expert_ids[:, :, None] == lax.iota(jnp.int32, E)
    named = jnp.any(hit, axis=1)
    counts = jnp.sum(named.astype(jnp.int32), axis=0).reshape(num_gx, local)
    needed = jnp.max(jnp.sum(counts, axis=1))
    earlier = lax.iota(jnp.int32, local)[:, None] < lax.iota(jnp.int32, local)[None, :]
    starts = jnp.sum(jnp.where(earlier[None], counts[:, :, None], 0), axis=1)
    mine = group_index * local + lax.iota(jnp.int32, local)
    hit_mine = expert_ids[:, :, None] == mine
    mine_named = jnp.any(hit_mine, axis=1)
    weight = jnp.sum(jnp.where(hit_mine, mixing[:, :, None], 0.0), axis=1)
    requests = expert_ids.shape[0]
    before = (lax.iota(jnp.int32, requests)[None, :] < lax.iota(jnp.int32, requests)[:, None])
    rank = jnp.dot(
        before.astype(bf16), mine_named.astype(bf16), preferred_element_type=f32
    ).astype(jnp.int32)
    start = lax.dynamic_index_in_dim(starts, group_index, 0, False)
    place = jnp.where(mine_named, rank + start[None, :], -1)
    base = start // ALIGN * ALIGN
    rank = jnp.where(mine_named, place - base[None, :], -1)
    return rank, place, weight, base, needed


def dispatch_kernel(h_ref, gain_ref, rank_ref, x_ref, square_ref):
    slots = x_ref.shape[1]
    h = h_ref[...].astype(f32)
    square_ref[...] = lax.dot_general(
        jnp.ones((8, h.shape[1]), f32),
        h * h,
        (((1,), (1,)), ((), ())),
        precision=lax.Precision.HIGHEST,
        preferred_element_type=f32,
    )
    scaled = (h * gain_ref[...].astype(f32)).astype(bf16)
    slot = lax.broadcasted_iota(jnp.int32, (slots, h.shape[0]), 0)
    for e in range(x_ref.shape[0]):
        pick = (rank_ref[e : e + 1, :] == slot).astype(f32).astype(bf16)
        x_ref[e] = jnp.dot(pick, scaled, preferred_element_type=f32).astype(bf16)


def dispatch(hidden_all, gain, rank_t, slots):
    requests, features = hidden_all.shape
    return pl.pallas_call(
        dispatch_kernel,
        out_shape=(
            jax.ShapeDtypeStruct((rank_t.shape[0], slots, features), bf16),
            jax.ShapeDtypeStruct((8, requests), f32),
        ),
        compiler_params=params(6),
        name="dispatch",
    )(hidden_all, gain.reshape(1, -1), rank_t)


def gate_up_kernel(bit, chunk, me_s, base_s, x_ref, w_hbm, keep_ref, send_ref, scr, buf, sem):
    experts, slots, _ = x_ref.shape
    units = buf.shape[3]
    hidden_units = units * CHUNKS

    def copies(e):
        return [
            pltpu.make_async_copy(
                w_hbm.at[e, :, pl.ds(half * hidden_units + chunk * units, units)],
                buf.at[e, half],
                sem.at[e, half],
            )
            for half in range(2)
        ]

    for e in range(experts):
        for copy in copies(e):
            copy.start()
    scr[...] = jnp.zeros(scr.shape, f32)
    unroll = min(UNROLL, experts)

    def visit(step, carry):
        these = [step * unroll + i for i in range(unroll)]
        for e in these:
            for copy in copies(e):
                copy.wait()
        products = [
            [jnp.dot(x_ref[e], buf[e, half], preferred_element_type=f32) for half in range(2)]
            for e in these
        ]
        for e, pair in zip(these, products):
            rows = pl.ds(pl.multiple_of(base_s[e], ALIGN), slots)
            for half in range(2):
                scr[rows, half * units : (half + 1) * units] += pair[half]
        return carry

    lax.fori_loop(0, experts // unroll, visit, 0)
    half, each, _ = keep_ref.shape
    me = me_s[0]
    for i in range(half):
        other = (i // bit) * 2 * bit + i % bit
        at = jnp.bitwise_xor(me, other) * each
        keep_ref[i] = scr[pl.ds(pl.multiple_of(at, ALIGN), each), :].astype(bf16)
        at = jnp.bitwise_xor(me, other + bit) * each
        send_ref[i] = scr[pl.ds(pl.multiple_of(at, ALIGN), each), :].astype(bf16)


def gate_up(x, w_gate_up, base, me, capacity, parts, chunk, bit):
    experts, slots, features = x.shape
    units = w_gate_up.shape[2] // (2 * CHUNKS)
    out = jax.ShapeDtypeStruct((parts // 2, capacity // parts, 2 * units), bf16)
    return pl.pallas_call(
        functools.partial(gate_up_kernel, bit, chunk),
        out_shape=(out, out),
        grid_spec=pltpu.PrefetchScalarGridSpec(
            num_scalar_prefetch=2,
            grid=(1,),
            in_specs=[whole(x.shape), pl.BlockSpec(memory_space=pltpu.HBM)],
            out_specs=(whole(out.shape), whole(out.shape)),
            scratch_shapes=[
                pltpu.VMEM((capacity + slots, 2 * units), f32),
                pltpu.VMEM((experts, 2, features, units), bf16),
                pltpu.SemaphoreType.DMA((experts, 2)),
            ],
        ),
        compiler_params=params(40),
        cost_estimate=pl.CostEstimate(
            flops=4 * experts * slots * features * units,
            bytes_accessed=experts * features * units * 4 + out.size * 4,
            transcendentals=0,
        ),
        name="gate_up",
    )(me, base, x, w_gate_up)


def exchange(x, k, parts):
    return lax.ppermute(x, "gy", [(i, i ^ k) for i in range(parts)])


def scatter_sums(keep, send, order, parts):
    names = [k for k in range(parts) if not k & order[0]]
    total = keep.astype(f32) + exchange(send, order[0], parts).astype(f32)
    for k in order[1:]:
        kept = [i for i, n in enumerate(names) if not n & k]
        sent = [i for i, n in enumerate(names) if n & k]
        rest = jnp.stack([total[i] for i in sent]).astype(bf16)
        total = jnp.stack([total[i] for i in kept]) + exchange(rest, k, parts).astype(f32)
        names = [names[i] for i in kept]
    return total[0]


def gather_rows(x, order, parts):
    names = [0]
    x = x[None]
    for k in order[:-1]:
        x = jnp.concatenate([x, exchange(x, k, parts)], axis=0)
        names = names + [n ^ k for n in names]
    return x, exchange(x, order[-1], parts), names, [n ^ order[-1] for n in names]


def down_kernel(names, me_s, base_s, *refs):
    acts = refs[: len(names)]
    high_ref, low_ref, w_hbm, out_ref, scr, rows_scr, buf, sem = refs[len(names) :]
    experts = buf.shape[0]
    each = acts[0].shape[1]
    capacity = 2 * acts[0].shape[0] * each
    slots = scr.shape[0] - capacity
    me = me_s[0]

    def fetch(e):
        return pltpu.make_async_copy(w_hbm.at[e], buf.at[e], sem.at[e])

    for e in range(experts):
        fetch(e).start()
    scr[capacity:, :] = jnp.zeros((slots, scr.shape[1]), f32)
    for a, (ref, ns) in enumerate(zip(acts, names)):
        units = ref.shape[2]
        lanes = slice((a // 2) * units, (a // 2 + 1) * units)
        for i, n in enumerate(ns):
            at = jnp.bitwise_xor(me, n) * each
            scr[pl.ds(pl.multiple_of(at, ALIGN), each), lanes] = ref[i].astype(f32)
    unroll = min(UNROLL, experts)

    def visit(step, carry):
        these = [step * unroll + i for i in range(unroll)]
        for e in these:
            fetch(e).wait()
        products = [
            lax.dot_general(
                scr[pl.ds(pl.multiple_of(base_s[e], ALIGN), slots), :].astype(bf16),
                buf[e],
                (((1,), (1,)), ((), ())),
                preferred_element_type=f32,
            ).astype(bf16)
            for e in these
        ]
        for e, product in zip(these, products):
            rows_scr[pl.ds(pl.multiple_of(e * slots, 16), slots), :] = product
        return carry

    lax.fori_loop(0, experts // unroll, visit, 0)
    rows = rows_scr[...]
    out_ref[...] = jnp.dot(high_ref[...], rows, preferred_element_type=f32) + jnp.dot(
        low_ref[...], rows, preferred_element_type=f32
    )


def down(acts, names, w_down_t, base, me, high, low):
    experts, features, hidden_units = w_down_t.shape
    capacity = acts[0].shape[0] * acts[0].shape[1] * 2
    slots = high.shape[1] // experts
    total = high.shape[0]
    return pl.pallas_call(
        functools.partial(down_kernel, names),
        out_shape=jax.ShapeDtypeStruct((total, features), f32),
        grid_spec=pltpu.PrefetchScalarGridSpec(
            num_scalar_prefetch=2,
            grid=(1,),
            in_specs=[whole(a.shape) for a in acts]
            + [whole(high.shape), whole(low.shape), pl.BlockSpec(memory_space=pltpu.HBM)],
            out_specs=whole((total, features)),
            scratch_shapes=[
                pltpu.VMEM((capacity + slots, hidden_units), f32),
                pltpu.VMEM((experts * slots, features), bf16),
                pltpu.VMEM(w_down_t.shape, bf16),
                pltpu.SemaphoreType.DMA((experts,)),
            ],
        ),
        compiler_params=params(26),
        name="down",
    )(me, base, *acts, high, low, w_down_t)


def plan_kernel(rank_ref, weight_ref, high_ref, low_ref):
    requests, experts = rank_ref.shape
    slots = high_ref.shape[1] // experts
    rank = rank_ref[...].astype(f32).astype(bf16)
    weight = weight_ref[...]
    weight_high = weight.astype(bf16)
    weight_low = (weight - weight_high.astype(f32)).astype(bf16)
    expert = lax.broadcasted_iota(jnp.int32, (experts, experts * slots), 0)
    column = lax.broadcasted_iota(jnp.int32, (experts, experts * slots), 1)
    spread = ((column >= expert * slots) & (column < (expert + 1) * slots)).astype(f32).astype(bf16)
    offset = jnp.sum(jnp.where(column >= expert * slots, 1, 0), axis=0, keepdims=True) - 1
    slot = column[0:1] - offset * slots

    def over(x):
        return jnp.dot(x, spread, preferred_element_type=f32)

    here = over(rank).astype(jnp.int32) == slot
    high_ref[...] = jnp.where(here, over(weight_high), 0.0).astype(bf16)
    low_ref[...] = jnp.where(here, over(weight_low), 0.0).astype(bf16)


def plan(rank, weight, slots):
    out = jax.ShapeDtypeStruct((rank.shape[0], rank.shape[1] * slots), bf16)
    return pl.pallas_call(
        plan_kernel, out_shape=(out, out), compiler_params=params(6), name="plan"
    )(rank, weight)


def sum_over_gy(x, parts):
    k = 1
    while k < parts:
        x = x + exchange(x, k, parts)
        k *= 2
    return x


def experts_part(capacity, x, square, w_gate_up, w_down_t, base, place, high, low, me, parts):
    units = w_down_t.shape[2] // CHUNKS
    rows = capacity // parts
    here = me[0] * rows + lax.iota(jnp.int32, rows)
    mine = jnp.any(place[None] == here[:, None, None], axis=2)
    bits = [1 << i for i in range(parts.bit_length() - 1)]
    acts, names = [], []
    scale = None
    for chunk in range(CHUNKS):
        order = bits if chunk % 2 == 0 else bits[1:] + bits[:1]
        keep, send = gate_up(x, w_gate_up, base, me, capacity, parts, chunk, order[0])
        both = scatter_sums(keep, send, order, parts)
        if scale is None:
            inv = lax.rsqrt(sum_over_gy(square, parts).reshape(-1) / D + EPSILON)
            scale = jnp.sum(jnp.where(mine, inv[None, :], 0.0), axis=1)[:, None]
        gate = both[:, :units] * scale
        up = both[:, units:] * scale
        act = (jax.nn.silu(gate) * up).astype(bf16)
        left, right, left_names, right_names = gather_rows(act, order[::-1], parts)
        acts += [left, right]
        names += [left_names, right_names]
    return down(acts, names, w_down_t, base, me, high, low)


def out_kernel(a_ref, w_ref, r_ref, o_ref):
    projected = lax.dot_general(
        a_ref[...], w_ref[...], (((1,), (1,)), ((), ())), preferred_element_type=f32
    )
    o_ref[...] = (r_ref[...].astype(f32) + projected).astype(bf16)


def project(attention, out_weight, residual):
    return pl.pallas_call(
        out_kernel,
        out_shape=jax.ShapeDtypeStruct(residual.shape, bf16),
        compiler_params=params(8),
        name="project",
    )(attention, out_weight, residual)


def shards(
    queries,
    token_key_value,
    group_cached_keys,
    group_cached_values,
    owners,
    out_weight,
    residual,
    norm_gain,
    expert_ids,
    gate_logits,
    w_gate_up,
    w_down,
):
    rows, width = queries.shape
    parts = lax.axis_size("gy")
    num_gx = lax.axis_size("gx")
    me_y = lax.axis_index("gy")
    me_x = lax.axis_index("gx")
    me = jnp.full((1,), me_y, jnp.int32)
    each = rows // parts
    slots = -(-(num_gx * CAPS + ALIGN - 1) // 16) * 16
    local = w_gate_up.shape[0]

    part = attend_local(queries, group_cached_keys, group_cached_values, owners, parts)
    part = lax.all_to_all(part, "gy", 0, 0)
    attention = merge(
        part,
        lax.dynamic_slice_in_dim(queries, me_y * each, each, 0),
        lax.dynamic_slice_in_dim(token_key_value, me_y * each, each, 0),
    )
    attention = lax.all_to_all(
        jnp.broadcast_to(attention[None], (parts,) + attention.shape), "gy", 0, 0
    ).reshape(rows, width)
    hidden = project(attention, out_weight.T, residual)
    hidden_all = lax.all_gather(hidden, "gx", axis=0, tiled=True)

    mixing = jax.nn.softmax(gate_logits, axis=-1)
    rank, place, weight, base, needed = routing(expert_ids, mixing, num_gx, me_x)
    high, low = plan(rank, weight, slots)
    x, square = dispatch(hidden_all, norm_gain, rank.T, slots)

    capacity = local * num_gx * CAPS
    sizes = [c for c in (448, 512) if c < capacity and c % (ALIGN * parts) == 0] + [capacity]
    branch = sum((needed > c).astype(jnp.int32) for c in sizes[:-1])
    operands = (
        x,
        square[0].reshape(-1, 128),
        w_gate_up,
        jnp.swapaxes(w_down, 1, 2),
        base,
        place,
        high,
        low,
        me,
    )
    routed = lax.switch(
        branch,
        [lambda *o, c=c: experts_part(c, *o, parts=parts) for c in sizes],
        *operands,
    )
    routed = lax.all_to_all(routed.reshape(num_gx, rows, -1), "gx", 0, 0)
    return hidden.astype(f32) + jnp.sum(routed, axis=0)


def solution(mesh):
    placed = (
        P("gx", None),
        P("gx", None),
        P("gx", "gy", None),
        P("gx", "gy", None),
        P("gx", "gy"),
        P(None, "gy"),
        P("gx", "gy"),
        P("gy"),
        P(),
        P(),
        P("gx", "gy", None),
        P("gx", None, "gy"),
    )
    return jax.shard_map(
        shards, mesh=mesh, in_specs=placed, out_specs=P("gx", "gy"), check_vma=False
    )
```

```python
import functools

import jax
import jax.numpy as jnp
from jax import lax
from jax.experimental import pallas as pl
from jax.experimental.pallas import tpu as pltpu
from jax.sharding import PartitionSpec as P

D = 2560
QUERY_HEADS = 20
KEY_VALUE_HEADS = 4
HEAD_SIZE = 128
GROUP = QUERY_HEADS // KEY_VALUE_HEADS
E = 64
TOPK = 6
CAPS = 12

LOWEST = -1e30
EPSILON = 1e-05
SCALING = HEAD_SIZE ** (-0.5)
BLOCK = 1024
ROWS = 16
ALIGN = 8
CHUNKS = 4
UNROLL = 2

f32 = jnp.float32
bf16 = jnp.bfloat16
MIB = 1024 * 1024


def params(mib):
    return pltpu.CompilerParams(vmem_limit_bytes=mib * MIB)


def whole(shape):
    return pl.BlockSpec(shape, lambda *_: (0,) * len(shape))


def attend_kernel(
    owner_s, q_ref, own_ref, k_hbm, v_hbm, out_ref, k_scr, v_scr, q_scr, m_scr, l_scr, acc_scr, sem
):
    groups = q_scr.shape[0]
    blocks = sem.shape[1]
    block = k_scr.shape[0] // blocks

    def copies(b):
        rows = pl.ds(b * block, block)
        return (
            pltpu.make_async_copy(k_hbm.at[0, rows], k_scr.at[rows], sem.at[0, b]),
            pltpu.make_async_copy(v_hbm.at[0, rows], v_scr.at[rows], sem.at[1, b]),
        )

    for b in range(blocks):
        for copy in copies(b):
            copy.start()
    for rg in range(groups):
        for c in range(KEY_VALUE_HEADS):
            for g in range(GROUP):
                h = c * GROUP + g
                q_scr[rg, c, g * ROWS : (g + 1) * ROWS, :] = q_ref[
                    rg * ROWS : (rg + 1) * ROWS, h * HEAD_SIZE : (h + 1) * HEAD_SIZE
                ]
    m_scr[...] = jnp.full(m_scr.shape, LOWEST, f32)
    l_scr[...] = jnp.zeros(l_scr.shape, f32)
    acc_scr[...] = jnp.zeros(acc_scr.shape, f32)
    heads = range(KEY_VALUE_HEADS)
    lanes = [slice(c * HEAD_SIZE, (c + 1) * HEAD_SIZE) for c in heads]

    def walk(b, carry):
        for copy in copies(b):
            copy.wait()
        at = pl.multiple_of(b * block, block)
        rows = pl.ds(at, block)
        owner = own_ref[0:1, rows]

        def visit(rg, carry):
            ids = rg * ROWS + lax.broadcasted_iota(jnp.int32, (ROWS, block), 0)
            member = owner == ids
            states = [(m_scr[rg, c], l_scr[rg, c], acc_scr[rg, c]) for c in heads]
            scores = [
                lax.dot_general(
                    q_scr[rg, c],
                    k_scr[rows, lanes[c]],
                    (((1,), (1,)), ((), ())),
                    preferred_element_type=f32,
                )
                * SCALING
                for c in heads
            ]
            results = []
            for c in heads:
                s = jnp.where(member[None], scores[c].reshape(GROUP, ROWS, block), LOWEST)
                s = s.reshape(GROUP * ROWS, block)
                m_old, l_old, acc_old = states[c]
                m_new = jnp.maximum(m_old, jnp.max(s, axis=1, keepdims=True))
                alpha = jnp.exp(m_old - m_new)
                p = jnp.exp(s - m_new[:, :1]).astype(bf16)
                l_new = l_old * alpha + jnp.sum(p.astype(f32), axis=1, keepdims=True)
                acc_new = acc_old * alpha + jnp.dot(
                    p, v_scr[rows, lanes[c]], preferred_element_type=f32
                )
                results.append((m_new, l_new, acc_new))
            for c in heads:
                m_scr[rg, c], l_scr[rg, c], acc_scr[rg, c] = results[c]
            return carry

        first = owner_s[at] // ROWS
        last = owner_s[at + block - 1] // ROWS
        return lax.fori_loop(first, last + 1, visit, carry)

    lax.fori_loop(0, blocks, walk, 0)

    width = QUERY_HEADS * HEAD_SIZE
    lane = lax.broadcasted_iota(jnp.int32, (ROWS, 128), 1)
    piece = lane % 3
    per = out_ref.shape[1]
    for rg in range(groups):

        def put(value, lanes):
            if per >= ROWS:
                at = rg * ROWS
                out_ref[at // per, at % per : at % per + ROWS, lanes] = value.astype(bf16)
            else:
                for i in range(ROWS // per):
                    out_ref[(rg * ROWS) // per + i, :, lanes] = value[
                        i * per : (i + 1) * per
                    ].astype(bf16)

        tail = jnp.zeros((ROWS, 128), f32)
        for c in heads:
            for g in range(GROUP):
                h = c * GROUP + g
                rows = slice(g * ROWS, (g + 1) * ROWS)
                m = m_scr[rg, c, rows, :]
                l = l_scr[rg, c, rows, :]
                tail = jnp.where(lane // 6 == h, jnp.where(lane % 6 < 3, m, l), tail)
                put(
                    acc_scr[rg, c, rows, :] / jnp.maximum(l, 1e-30),
                    slice(h * HEAD_SIZE, (h + 1) * HEAD_SIZE),
                )
        high = tail.astype(bf16).astype(f32)
        rest = tail - high
        middle = rest.astype(bf16).astype(f32)
        low = (rest - middle).astype(bf16).astype(f32)
        put(
            jnp.where(piece == 0, high, jnp.where(piece == 1, middle, low)),
            slice(width, width + 128),
        )


def attend_local(queries, keys, values, owners, parts):
    rows, width = queries.shape
    positions, kv = keys.shape[1:]
    block = min(BLOCK, positions)
    groups = rows // ROWS
    state = (groups, KEY_VALUE_HEADS, GROUP * ROWS, 128)
    out = jax.ShapeDtypeStruct((parts, rows // parts, width + 128), bf16)
    return pl.pallas_call(
        attend_kernel,
        out_shape=out,
        grid_spec=pltpu.PrefetchScalarGridSpec(
            num_scalar_prefetch=1,
            grid=(1,),
            in_specs=[
                whole((rows, width)),
                whole((1, positions)),
                pl.BlockSpec(memory_space=pltpu.HBM),
                pl.BlockSpec(memory_space=pltpu.HBM),
            ],
            out_specs=whole(out.shape),
            scratch_shapes=[
                pltpu.VMEM((positions, kv), bf16),
                pltpu.VMEM((positions, kv), bf16),
                pltpu.VMEM((groups, KEY_VALUE_HEADS, GROUP * ROWS, HEAD_SIZE), bf16),
                pltpu.VMEM(state, f32),
                pltpu.VMEM(state, f32),
                pltpu.VMEM(state, f32),
                pltpu.SemaphoreType.DMA((2, positions // block)),
            ],
        ),
        compiler_params=params(56),
        name="attend",
    )(owners.reshape(-1), queries, owners, keys, values)


def merge_kernel(part_ref, q_ref, kv_ref, out_ref):
    parts, rows, _ = part_ref.shape
    width = QUERY_HEADS * HEAD_SIZE
    kv = KEY_VALUE_HEADS * HEAD_SIZE
    source = lax.broadcasted_iota(jnp.int32, (128, 256), 0)
    target = lax.broadcasted_iota(jnp.int32, (128, 256), 1)
    wanted = (target % 128) * 6 + (target // 128) * 3
    pick = jnp.where(
        (source >= wanted) & (source < wanted + 3) & (target % 128 < QUERY_HEADS), 1.0, 0.0
    ).astype(bf16)
    lane = lax.broadcasted_iota(jnp.int32, (rows, 128), 1)
    own = jnp.zeros((rows, 128), f32)
    for h in range(QUERY_HEADS):
        c = h // GROUP
        product = q_ref[:, h * HEAD_SIZE : (h + 1) * HEAD_SIZE].astype(f32) * kv_ref[
            :, c * HEAD_SIZE : (c + 1) * HEAD_SIZE
        ].astype(f32)
        own = jnp.where(lane == h, jnp.sum(product, axis=1, keepdims=True) * SCALING, own)
    maxima, sums = [], []
    peak = own
    for j in range(parts):
        both = jnp.dot(part_ref[j, :, width:], pick, preferred_element_type=f32)
        maxima.append(both[:, :128])
        sums.append(both[:, 128:])
        peak = jnp.maximum(peak, both[:, :128])
    own_prob = jnp.exp(own - peak).astype(bf16).astype(f32)
    weights = [l * jnp.exp(m - peak) for m, l in zip(maxima, sums)]
    den = own_prob
    for w in weights:
        den = den + w
    own_prob = own_prob / den
    weights = [w / den for w in weights]
    for h in range(QUERY_HEADS):
        c = h // GROUP
        lanes = slice(h * HEAD_SIZE, (h + 1) * HEAD_SIZE)
        acc = own_prob[:, h : h + 1] * kv_ref[
            :, kv + c * HEAD_SIZE : kv + (c + 1) * HEAD_SIZE
        ].astype(f32)
        for j in range(parts):
            acc = acc + weights[j][:, h : h + 1] * part_ref[j, :, lanes].astype(f32)
        out_ref[:, lanes] = acc.astype(bf16)


def merge(part, queries, token_key_value):
    return pl.pallas_call(
        merge_kernel,
        out_shape=jax.ShapeDtypeStruct(queries.shape, bf16),
        compiler_params=params(6),
        name="merge",
    )(part, queries, token_key_value)


def routing(expert_ids, mixing, num_gx, group_index):
    local = E // num_gx
    hit = expert_ids[:, :, None] == lax.iota(jnp.int32, E)
    named = jnp.any(hit, axis=1)
    counts = jnp.sum(named.astype(jnp.int32), axis=0).reshape(num_gx, local)
    needed = jnp.max(jnp.sum(counts, axis=1))
    earlier = lax.iota(jnp.int32, local)[:, None] < lax.iota(jnp.int32, local)[None, :]
    starts = jnp.sum(jnp.where(earlier[None], counts[:, :, None], 0), axis=1)
    mine = group_index * local + lax.iota(jnp.int32, local)
    hit_mine = expert_ids[:, :, None] == mine
    mine_named = jnp.any(hit_mine, axis=1)
    weight = jnp.sum(jnp.where(hit_mine, mixing[:, :, None], 0.0), axis=1)
    requests = expert_ids.shape[0]
    before = (lax.iota(jnp.int32, requests)[None, :] < lax.iota(jnp.int32, requests)[:, None])
    rank = jnp.dot(
        before.astype(bf16), mine_named.astype(bf16), preferred_element_type=f32
    ).astype(jnp.int32)
    start = lax.dynamic_index_in_dim(starts, group_index, 0, False)
    place = jnp.where(mine_named, rank + start[None, :], -1)
    base = start // ALIGN * ALIGN
    rank = jnp.where(mine_named, place - base[None, :], -1)
    return rank, place, weight, base, needed


def dispatch_kernel(h_ref, gain_ref, rank_ref, x_ref, square_ref):
    slots = x_ref.shape[1]
    h = h_ref[...].astype(f32)
    square_ref[...] = lax.dot_general(
        jnp.ones((8, h.shape[1]), f32),
        h * h,
        (((1,), (1,)), ((), ())),
        precision=lax.Precision.HIGHEST,
        preferred_element_type=f32,
    )
    scaled = (h * gain_ref[...].astype(f32)).astype(bf16)
    slot = lax.broadcasted_iota(jnp.int32, (slots, h.shape[0]), 0)
    for e in range(x_ref.shape[0]):
        pick = (rank_ref[e : e + 1, :] == slot).astype(f32).astype(bf16)
        x_ref[e] = jnp.dot(pick, scaled, preferred_element_type=f32).astype(bf16)


def dispatch(hidden_all, gain, rank_t, slots):
    requests, features = hidden_all.shape
    return pl.pallas_call(
        dispatch_kernel,
        out_shape=(
            jax.ShapeDtypeStruct((rank_t.shape[0], slots, features), bf16),
            jax.ShapeDtypeStruct((8, requests), f32),
        ),
        compiler_params=params(6),
        name="dispatch",
    )(hidden_all, gain.reshape(1, -1), rank_t)


def gate_up_kernel(names, bit, chunk, me_s, base_s, x_ref, w_hbm, keep_ref, send_ref, scr, buf, sem):
    experts, slots, _ = x_ref.shape
    units = buf.shape[3]
    hidden_units = units * CHUNKS

    def copies(e):
        return [
            pltpu.make_async_copy(
                w_hbm.at[e, :, pl.ds(half * hidden_units + chunk * units, units)],
                buf.at[e, half],
                sem.at[e, half],
            )
            for half in range(2)
        ]

    for e in range(experts):
        for copy in copies(e):
            copy.start()
    scr[...] = jnp.zeros(scr.shape, f32)
    unroll = min(UNROLL, experts)

    def visit(step, carry):
        these = [step * unroll + i for i in range(unroll)]
        for e in these:
            for copy in copies(e):
                copy.wait()
        products = [
            [jnp.dot(x_ref[e], buf[e, half], preferred_element_type=f32) for half in range(2)]
            for e in these
        ]
        for e, pair in zip(these, products):
            rows = pl.ds(pl.multiple_of(base_s[e], ALIGN), slots)
            for half in range(2):
                scr[rows, half * units : (half + 1) * units] += pair[half]
        return carry

    lax.fori_loop(0, experts // unroll, visit, 0)
    each = keep_ref.shape[1]
    me = me_s[0]
    for i, name in enumerate(names):
        at = jnp.bitwise_xor(me, name) * each
        keep_ref[i] = scr[pl.ds(pl.multiple_of(at, ALIGN), each), :].astype(bf16)
        at = jnp.bitwise_xor(me, name ^ bit) * each
        send_ref[i] = scr[pl.ds(pl.multiple_of(at, ALIGN), each), :].astype(bf16)


def gate_up(x, w_gate_up, base, me, capacity, parts, chunk, names, bit):
    experts, slots, features = x.shape
    units = w_gate_up.shape[2] // (2 * CHUNKS)
    out = jax.ShapeDtypeStruct((parts // 2, capacity // parts, 2 * units), bf16)
    return pl.pallas_call(
        functools.partial(gate_up_kernel, names, bit, chunk),
        out_shape=(out, out),
        grid_spec=pltpu.PrefetchScalarGridSpec(
            num_scalar_prefetch=2,
            grid=(1,),
            in_specs=[whole(x.shape), pl.BlockSpec(memory_space=pltpu.HBM)],
            out_specs=(whole(out.shape), whole(out.shape)),
            scratch_shapes=[
                pltpu.VMEM((capacity + slots, 2 * units), f32),
                pltpu.VMEM((experts, 2, features, units), bf16),
                pltpu.SemaphoreType.DMA((experts, 2)),
            ],
        ),
        compiler_params=params(40),
        cost_estimate=pl.CostEstimate(
            flops=4 * experts * slots * features * units,
            bytes_accessed=experts * features * units * 4 + out.size * 4,
            transcendentals=0,
        ),
        name="gate_up",
    )(me, base, x, w_gate_up)


def exchange(x, k, parts):
    return lax.ppermute(x, "gy", [(i, i ^ k) for i in range(parts)])


def down_kernel(names, me_s, base_s, *refs):
    acts = refs[: len(names)]
    high_ref, low_ref, w_ref, out_ref, scr, rows_scr = refs[len(names) :]
    experts = w_ref.shape[0]
    each = acts[0].shape[1]
    capacity = 2 * acts[0].shape[0] * each
    slots = scr.shape[0] - capacity
    me = me_s[0]

    scr[capacity:, :] = jnp.zeros((slots, scr.shape[1]), f32)
    for a, (ref, ns) in enumerate(zip(acts, names)):
        units = ref.shape[2]
        lanes = slice((a // 2) * units, (a // 2 + 1) * units)
        for i, n in enumerate(ns):
            at = jnp.bitwise_xor(me, n) * each
            scr[pl.ds(pl.multiple_of(at, ALIGN), each), lanes] = ref[i].astype(f32)
    unroll = min(UNROLL, experts)

    def visit(step, carry):
        these = [step * unroll + i for i in range(unroll)]
        products = [
            lax.dot_general(
                scr[pl.ds(pl.multiple_of(base_s[e], ALIGN), slots), :].astype(bf16),
                w_ref[e],
                (((1,), (1,)), ((), ())),
                preferred_element_type=f32,
            ).astype(bf16)
            for e in these
        ]
        for e, product in zip(these, products):
            rows_scr[pl.ds(pl.multiple_of(e * slots, 16), slots), :] = product
        return carry

    lax.fori_loop(0, experts // unroll, visit, 0)
    rows = rows_scr[...]
    out_ref[...] = jnp.dot(high_ref[...], rows, preferred_element_type=f32) + jnp.dot(
        low_ref[...], rows, preferred_element_type=f32
    )


def down(acts, names, w_down_t, base, me, high, low):
    experts, features, hidden_units = w_down_t.shape
    capacity = acts[0].shape[0] * acts[0].shape[1] * 2
    slots = high.shape[1] // experts
    total = high.shape[0]
    return pl.pallas_call(
        functools.partial(down_kernel, names),
        out_shape=jax.ShapeDtypeStruct((total, features), f32),
        grid_spec=pltpu.PrefetchScalarGridSpec(
            num_scalar_prefetch=2,
            grid=(1,),
            in_specs=[whole(a.shape) for a in acts]
            + [whole(high.shape), whole(low.shape), pl.BlockSpec(memory_space=pltpu.VMEM)],
            out_specs=whole((total, features)),
            scratch_shapes=[
                pltpu.VMEM((capacity + slots, hidden_units), f32),
                pltpu.VMEM((experts * slots, features), bf16),
            ],
        ),
        compiler_params=params(26),
        name="down",
    )(me, base, *acts, high, low, w_down_t)


def plan_kernel(rank_ref, weight_ref, high_ref, low_ref):
    requests, experts = rank_ref.shape
    slots = high_ref.shape[1] // experts
    rank = rank_ref[...].astype(f32).astype(bf16)
    weight = weight_ref[...]
    weight_high = weight.astype(bf16)
    weight_low = (weight - weight_high.astype(f32)).astype(bf16)
    expert = lax.broadcasted_iota(jnp.int32, (experts, experts * slots), 0)
    column = lax.broadcasted_iota(jnp.int32, (experts, experts * slots), 1)
    spread = ((column >= expert * slots) & (column < (expert + 1) * slots)).astype(f32).astype(bf16)
    offset = jnp.sum(jnp.where(column >= expert * slots, 1, 0), axis=0, keepdims=True) - 1
    slot = column[0:1] - offset * slots

    def over(x):
        return jnp.dot(x, spread, preferred_element_type=f32)

    here = over(rank).astype(jnp.int32) == slot
    high_ref[...] = jnp.where(here, over(weight_high), 0.0).astype(bf16)
    low_ref[...] = jnp.where(here, over(weight_low), 0.0).astype(bf16)


def plan(rank, weight, slots):
    out = jax.ShapeDtypeStruct((rank.shape[0], rank.shape[1] * slots), bf16)
    return pl.pallas_call(
        plan_kernel, out_shape=(out, out), compiler_params=params(6), name="plan"
    )(rank, weight)


def experts_part(capacity, x, square, w_gate_up, w_down_t, base, place, high, low, me, parts):
    units = w_down_t.shape[2] // CHUNKS
    rows = capacity // parts
    here = me[0] * rows + lax.iota(jnp.int32, rows)
    mine = jnp.any(place[None] == here[:, None, None], axis=2)
    bits = [1 << i for i in range(parts.bit_length() - 1)]
    last_token = [me]
    squares = [square]
    chunks = [dict() for _ in range(CHUNKS)]

    def after(*values):
        return lax.optimization_barrier((*values, last_token[0]))[:-1]

    def send(value, k):
        last_token[0] = value
        return exchange(value, k, parts)

    def add_squares():
        done = len(squares) - 1
        if done < len(bits):
            (value,) = after(squares[-1])
            squares.append(value + send(value, bits[done]))

    places = [0]
    for k in bits[:0:-1]:
        places = places + [n ^ k for n in places]

    def start(chunk, state):
        (ordered,) = after(base)
        keep, away = gate_up(
            x, w_gate_up, ordered, me, capacity, parts, chunk, places, bits[0]
        )
        state.update(total=keep, got=send(away, bits[0]))
        add_squares()

    def fold(k):
        def run(chunk, state):
            total, got = after(state["total"], state["got"])
            half = got.shape[0] // 2
            rest = (total[half:].astype(f32) + got[half:].astype(f32)).astype(bf16)
            state.update(
                total=total[:half].astype(f32) + got[:half].astype(f32), got=send(rest, k)
            )

        return run

    def activate(chunk, state):
        while len(squares) <= len(bits):
            add_squares()
        total, got = after(state["total"], state["got"])
        inv = lax.rsqrt(squares[-1].reshape(-1) / D + EPSILON)
        scale = jnp.sum(jnp.where(mine, inv[None, :], 0.0), axis=1)[:, None]
        both = total[0].astype(f32) + got[0].astype(f32)
        gate = both[:, :units] * scale
        up = both[:, units:] * scale
        act = (jax.nn.silu(gate) * up).astype(bf16)[None]
        state.update(left=act, right=send(act, bits[-1]), names=[0], last=bits[-1])

    def spread(k):
        def run(chunk, state):
            left, right = after(state["left"], state["right"])
            both = jnp.concatenate([left, right], axis=0)
            names = state["names"] + [n ^ state["last"] for n in state["names"]]
            state.update(left=both, right=send(both, k), names=names, last=k)

        return run

    stages = [start] + [fold(k) for k in bits[1:]] + [activate] + [spread(k) for k in bits[-2::-1]]
    for slot in range(CHUNKS + len(stages) - 1):
        for i, stage in enumerate(stages):
            if 0 <= slot - i < CHUNKS:
                stage(slot - i, chunks[slot - i])
    acts, names = [], []
    for state in chunks:
        acts += [state["left"], state["right"]]
        names += [state["names"], [n ^ state["last"] for n in state["names"]]]
    return down(acts, names, w_down_t, base, me, high, low)


def out_kernel(a_ref, w_ref, r_ref, o_ref):
    projected = lax.dot_general(
        a_ref[...], w_ref[...], (((1,), (1,)), ((), ())), preferred_element_type=f32
    )
    o_ref[...] = (r_ref[...].astype(f32) + projected).astype(bf16)


def project(attention, out_weight, residual):
    return pl.pallas_call(
        out_kernel,
        out_shape=jax.ShapeDtypeStruct(residual.shape, bf16),
        compiler_params=params(8),
        name="project",
    )(attention, out_weight, residual)


def shards(
    queries,
    token_key_value,
    group_cached_keys,
    group_cached_values,
    owners,
    out_weight,
    residual,
    norm_gain,
    expert_ids,
    gate_logits,
    w_gate_up,
    w_down,
):
    rows, width = queries.shape
    parts = lax.axis_size("gy")
    num_gx = lax.axis_size("gx")
    me_y = lax.axis_index("gy")
    me_x = lax.axis_index("gx")
    me = jnp.full((1,), me_y, jnp.int32)
    each = rows // parts
    slots = -(-(num_gx * CAPS + ALIGN - 1) // 16) * 16
    local = w_gate_up.shape[0]

    part = attend_local(queries, group_cached_keys, group_cached_values, owners, parts)
    part = lax.all_to_all(part, "gy", 0, 0)
    attention = merge(
        part,
        lax.dynamic_slice_in_dim(queries, me_y * each, each, 0),
        lax.dynamic_slice_in_dim(token_key_value, me_y * each, each, 0),
    )
    attention = lax.all_to_all(
        jnp.broadcast_to(attention[None], (parts,) + attention.shape), "gy", 0, 0
    ).reshape(rows, width)
    hidden = project(attention, out_weight.T, residual)
    hidden_all = lax.all_gather(hidden, "gx", axis=0, tiled=True)

    mixing = jax.nn.softmax(gate_logits, axis=-1)
    rank, place, weight, base, needed = routing(expert_ids, mixing, num_gx, me_x)
    high, low = plan(rank, weight, slots)
    x, square = dispatch(hidden_all, norm_gain, rank.T, slots)

    capacity = local * num_gx * CAPS
    sizes = [c for c in (448, 512) if c < capacity and c % (ALIGN * parts) == 0] + [capacity]
    branch = sum((needed > c).astype(jnp.int32) for c in sizes[:-1])
    operands = (
        x,
        square[0].reshape(-1, 128),
        w_gate_up,
        jnp.swapaxes(w_down, 1, 2),
        base,
        place,
        high,
        low,
        me,
    )
    routed = lax.switch(
        branch,
        [lambda *o, c=c: experts_part(c, *o, parts=parts) for c in sizes],
        *operands,
    )
    routed = lax.all_to_all(routed.reshape(num_gx, rows, -1), "gx", 0, 0)
    return hidden.astype(f32) + jnp.sum(routed, axis=0)


def solution(mesh):
    placed = (
        P("gx", None),
        P("gx", None),
        P("gx", "gy", None),
        P("gx", "gy", None),
        P("gx", "gy"),
        P(None, "gy"),
        P("gx", "gy"),
        P("gy"),
        P(),
        P(),
        P("gx", "gy", None),
        P("gx", None, "gy"),
    )
    return jax.shard_map(
        shards, mesh=mesh, in_specs=placed, out_specs=P("gx", "gy"), check_vma=False
    )
```

```python
import functools

import jax
import jax.numpy as jnp
from jax import lax
from jax.experimental import pallas as pl
from jax.experimental.pallas import tpu as pltpu
from jax.sharding import PartitionSpec as P

D = 2560
QUERY_HEADS = 20
KEY_VALUE_HEADS = 4
HEAD_SIZE = 128
GROUP = QUERY_HEADS // KEY_VALUE_HEADS
E = 64
TOPK = 6
CAPS = 12

LOWEST = -1e30
EPSILON = 1e-05
SCALING = HEAD_SIZE ** (-0.5)
BLOCK = 1024
ROWS = 16
ALIGN = 8
SHARES = (3, 3, 3, 3)
UNROLL = 4

f32 = jnp.float32
bf16 = jnp.bfloat16
MIB = 1024 * 1024


def params(mib):
    return pltpu.CompilerParams(vmem_limit_bytes=mib * MIB)


def whole(shape):
    return pl.BlockSpec(shape, lambda *_: (0,) * len(shape))


def attend_kernel(
    owner_s, q_ref, own_ref, k_hbm, v_hbm, out_ref, k_scr, v_scr, q_scr, m_scr, l_scr, acc_scr, sem
):
    groups = q_scr.shape[0]
    blocks = sem.shape[1]
    block = k_scr.shape[0] // blocks

    def copies(b):
        rows = pl.ds(b * block, block)
        return (
            pltpu.make_async_copy(k_hbm.at[0, rows], k_scr.at[rows], sem.at[0, b]),
            pltpu.make_async_copy(v_hbm.at[0, rows], v_scr.at[rows], sem.at[1, b]),
        )

    for b in range(blocks):
        for copy in copies(b):
            copy.start()
    for rg in range(groups):
        for c in range(KEY_VALUE_HEADS):
            for g in range(GROUP):
                h = c * GROUP + g
                q_scr[rg, c, g * ROWS : (g + 1) * ROWS, :] = q_ref[
                    rg * ROWS : (rg + 1) * ROWS, h * HEAD_SIZE : (h + 1) * HEAD_SIZE
                ]
    m_scr[...] = jnp.full(m_scr.shape, LOWEST, f32)
    l_scr[...] = jnp.zeros(l_scr.shape, f32)
    acc_scr[...] = jnp.zeros(acc_scr.shape, f32)
    heads = range(KEY_VALUE_HEADS)
    lanes = [slice(c * HEAD_SIZE, (c + 1) * HEAD_SIZE) for c in heads]

    def walk(b, carry):
        for copy in copies(b):
            copy.wait()
        at = pl.multiple_of(b * block, block)
        rows = pl.ds(at, block)
        owner = own_ref[0:1, rows]

        def visit(rg, carry):
            ids = rg * ROWS + lax.broadcasted_iota(jnp.int32, (ROWS, block), 0)
            member = owner == ids
            states = [(m_scr[rg, c], l_scr[rg, c], acc_scr[rg, c]) for c in heads]
            scores = [
                lax.dot_general(
                    q_scr[rg, c],
                    k_scr[rows, lanes[c]],
                    (((1,), (1,)), ((), ())),
                    preferred_element_type=f32,
                )
                * SCALING
                for c in heads
            ]
            results = []
            for c in heads:
                s = jnp.where(member[None], scores[c].reshape(GROUP, ROWS, block), LOWEST)
                s = s.reshape(GROUP * ROWS, block)
                m_old, l_old, acc_old = states[c]
                m_new = jnp.maximum(m_old, jnp.max(s, axis=1, keepdims=True))
                alpha = jnp.exp(m_old - m_new)
                p = jnp.exp(s - m_new[:, :1]).astype(bf16)
                l_new = l_old * alpha + jnp.sum(p.astype(f32), axis=1, keepdims=True)
                acc_new = acc_old * alpha + jnp.dot(
                    p, v_scr[rows, lanes[c]], preferred_element_type=f32
                )
                results.append((m_new, l_new, acc_new))
            for c in heads:
                m_scr[rg, c], l_scr[rg, c], acc_scr[rg, c] = results[c]
            return carry

        first = owner_s[at] // ROWS
        last = owner_s[at + block - 1] // ROWS
        return lax.fori_loop(first, last + 1, visit, carry)

    lax.fori_loop(0, blocks, walk, 0)

    width = QUERY_HEADS * HEAD_SIZE
    lane = lax.broadcasted_iota(jnp.int32, (ROWS, 128), 1)
    piece = lane % 3
    per = out_ref.shape[1]
    for rg in range(groups):

        def put(value, lanes):
            if per >= ROWS:
                at = rg * ROWS
                out_ref[at // per, at % per : at % per + ROWS, lanes] = value.astype(bf16)
            else:
                for i in range(ROWS // per):
                    out_ref[(rg * ROWS) // per + i, :, lanes] = value[
                        i * per : (i + 1) * per
                    ].astype(bf16)

        tail = jnp.zeros((ROWS, 128), f32)
        for c in heads:
            for g in range(GROUP):
                h = c * GROUP + g
                rows = slice(g * ROWS, (g + 1) * ROWS)
                m = m_scr[rg, c, rows, :]
                l = l_scr[rg, c, rows, :]
                tail = jnp.where(lane // 6 == h, jnp.where(lane % 6 < 3, m, l), tail)
                put(
                    acc_scr[rg, c, rows, :] / jnp.maximum(l, 1e-30),
                    slice(h * HEAD_SIZE, (h + 1) * HEAD_SIZE),
                )
        high = tail.astype(bf16).astype(f32)
        rest = tail - high
        middle = rest.astype(bf16).astype(f32)
        low = (rest - middle).astype(bf16).astype(f32)
        put(
            jnp.where(piece == 0, high, jnp.where(piece == 1, middle, low)),
            slice(width, width + 128),
        )


def attend_local(queries, keys, values, owners, parts):
    rows, width = queries.shape
    positions, kv = keys.shape[1:]
    block = min(BLOCK, positions)
    groups = rows // ROWS
    state = (groups, KEY_VALUE_HEADS, GROUP * ROWS, 128)
    out = jax.ShapeDtypeStruct((parts, rows // parts, width + 128), bf16)
    return pl.pallas_call(
        attend_kernel,
        out_shape=out,
        grid_spec=pltpu.PrefetchScalarGridSpec(
            num_scalar_prefetch=1,
            grid=(1,),
            in_specs=[
                whole((rows, width)),
                whole((1, positions)),
                pl.BlockSpec(memory_space=pltpu.HBM),
                pl.BlockSpec(memory_space=pltpu.HBM),
            ],
            out_specs=whole(out.shape),
            scratch_shapes=[
                pltpu.VMEM((positions, kv), bf16),
                pltpu.VMEM((positions, kv), bf16),
                pltpu.VMEM((groups, KEY_VALUE_HEADS, GROUP * ROWS, HEAD_SIZE), bf16),
                pltpu.VMEM(state, f32),
                pltpu.VMEM(state, f32),
                pltpu.VMEM(state, f32),
                pltpu.SemaphoreType.DMA((2, positions // block)),
            ],
        ),
        compiler_params=params(56),
        name="attend",
    )(owners.reshape(-1), queries, owners, keys, values)


def merge_kernel(part_ref, q_ref, kv_ref, out_ref):
    parts, rows, _ = part_ref.shape
    width = QUERY_HEADS * HEAD_SIZE
    kv = KEY_VALUE_HEADS * HEAD_SIZE
    source = lax.broadcasted_iota(jnp.int32, (128, 256), 0)
    target = lax.broadcasted_iota(jnp.int32, (128, 256), 1)
    wanted = (target % 128) * 6 + (target // 128) * 3
    pick = jnp.where(
        (source >= wanted) & (source < wanted + 3) & (target % 128 < QUERY_HEADS), 1.0, 0.0
    ).astype(bf16)
    lane = lax.broadcasted_iota(jnp.int32, (rows, 128), 1)
    own = jnp.zeros((rows, 128), f32)
    for h in range(QUERY_HEADS):
        c = h // GROUP
        product = q_ref[:, h * HEAD_SIZE : (h + 1) * HEAD_SIZE].astype(f32) * kv_ref[
            :, c * HEAD_SIZE : (c + 1) * HEAD_SIZE
        ].astype(f32)
        own = jnp.where(lane == h, jnp.sum(product, axis=1, keepdims=True) * SCALING, own)
    maxima, sums = [], []
    peak = own
    for j in range(parts):
        both = jnp.dot(part_ref[j, :, width:], pick, preferred_element_type=f32)
        maxima.append(both[:, :128])
        sums.append(both[:, 128:])
        peak = jnp.maximum(peak, both[:, :128])
    own_prob = jnp.exp(own - peak).astype(bf16).astype(f32)
    weights = [l * jnp.exp(m - peak) for m, l in zip(maxima, sums)]
    den = own_prob
    for w in weights:
        den = den + w
    own_prob = own_prob / den
    weights = [w / den for w in weights]
    for h in range(QUERY_HEADS):
        c = h // GROUP
        lanes = slice(h * HEAD_SIZE, (h + 1) * HEAD_SIZE)
        acc = own_prob[:, h : h + 1] * kv_ref[
            :, kv + c * HEAD_SIZE : kv + (c + 1) * HEAD_SIZE
        ].astype(f32)
        for j in range(parts):
            acc = acc + weights[j][:, h : h + 1] * part_ref[j, :, lanes].astype(f32)
        out_ref[:, lanes] = acc.astype(bf16)


def merge(part, queries, token_key_value):
    return pl.pallas_call(
        merge_kernel,
        out_shape=jax.ShapeDtypeStruct(queries.shape, bf16),
        compiler_params=params(6),
        name="merge",
    )(part, queries, token_key_value)


def routing(expert_ids, mixing, num_gx, group_index):
    local = E // num_gx
    hit = expert_ids[:, :, None] == lax.iota(jnp.int32, E)
    named = jnp.any(hit, axis=1)
    counts = jnp.sum(named.astype(jnp.int32), axis=0).reshape(num_gx, local)
    needed = jnp.max(jnp.sum(counts, axis=1))
    earlier = lax.iota(jnp.int32, local)[:, None] < lax.iota(jnp.int32, local)[None, :]
    starts = jnp.sum(jnp.where(earlier[None], counts[:, :, None], 0), axis=1)
    mine = group_index * local + lax.iota(jnp.int32, local)
    hit_mine = expert_ids[:, :, None] == mine
    mine_named = jnp.any(hit_mine, axis=1)
    weight = jnp.sum(jnp.where(hit_mine, mixing[:, :, None], 0.0), axis=1)
    requests = expert_ids.shape[0]
    before = (lax.iota(jnp.int32, requests)[None, :] < lax.iota(jnp.int32, requests)[:, None])
    rank = jnp.dot(
        before.astype(bf16), mine_named.astype(bf16), preferred_element_type=f32
    ).astype(jnp.int32)
    start = lax.dynamic_index_in_dim(starts, group_index, 0, False)
    place = jnp.where(mine_named, rank + start[None, :], -1)
    base = start // ALIGN * ALIGN
    rank = jnp.where(mine_named, place - base[None, :], -1)
    return rank, place, weight, base, needed


def dispatch_kernel(h_ref, gain_ref, rank_ref, x_ref, square_ref):
    slots = x_ref.shape[1]
    h = h_ref[...].astype(f32)
    square_ref[...] = lax.dot_general(
        jnp.ones((8, h.shape[1]), f32),
        h * h,
        (((1,), (1,)), ((), ())),
        precision=lax.Precision.HIGHEST,
        preferred_element_type=f32,
    )
    scaled = (h * gain_ref[...].astype(f32)).astype(bf16)
    slot = lax.broadcasted_iota(jnp.int32, (slots, h.shape[0]), 0)
    for e in range(x_ref.shape[0]):
        pick = (rank_ref[e : e + 1, :] == slot).astype(f32).astype(bf16)
        x_ref[e] = jnp.dot(pick, scaled, preferred_element_type=f32).astype(bf16)


def dispatch(hidden_all, gain, rank_t, slots):
    requests, features = hidden_all.shape
    return pl.pallas_call(
        dispatch_kernel,
        out_shape=(
            jax.ShapeDtypeStruct((rank_t.shape[0], slots, features), bf16),
            jax.ShapeDtypeStruct((8, requests), f32),
        ),
        compiler_params=params(6),
        name="dispatch",
    )(hidden_all, gain.reshape(1, -1), rank_t)


def gate_up_kernel(names, bit, first, hidden_units, me_s, base_s, x_ref, w_hbm, keep_ref, send_ref, scr, buf, sem):
    experts, slots, _ = x_ref.shape
    units = buf.shape[3]

    def copies(e):
        return [
            pltpu.make_async_copy(
                w_hbm.at[e, :, pl.ds(half * hidden_units + first, units)],
                buf.at[e, half],
                sem.at[e, half],
            )
            for half in range(2)
        ]

    for e in range(experts):
        for copy in copies(e):
            copy.start()
    scr[...] = jnp.zeros(scr.shape, f32)
    unroll = min(UNROLL, experts)

    def visit(step, carry):
        these = [step * unroll + i for i in range(unroll)]
        for e in these:
            for copy in copies(e):
                copy.wait()
        products = [
            [jnp.dot(x_ref[e], buf[e, half], preferred_element_type=f32) for half in range(2)]
            for e in these
        ]
        for e, pair in zip(these, products):
            rows = pl.ds(pl.multiple_of(base_s[e], ALIGN), slots)
            for half in range(2):
                scr[rows, half * units : (half + 1) * units] += pair[half]
        return carry

    lax.fori_loop(0, experts // unroll, visit, 0)
    each = keep_ref.shape[1]
    me = me_s[0]
    for i, name in enumerate(names):
        at = jnp.bitwise_xor(me, name) * each
        keep_ref[i] = scr[pl.ds(pl.multiple_of(at, ALIGN), each), :].astype(bf16)
        at = jnp.bitwise_xor(me, name ^ bit) * each
        send_ref[i] = scr[pl.ds(pl.multiple_of(at, ALIGN), each), :].astype(bf16)


def gate_up(x, w_gate_up, base, me, capacity, parts, first, units, names, bit):
    experts, slots, features = x.shape
    hidden_units = w_gate_up.shape[2] // 2
    out = jax.ShapeDtypeStruct((parts // 2, capacity // parts, 2 * units), bf16)
    return pl.pallas_call(
        functools.partial(gate_up_kernel, names, bit, first, hidden_units),
        out_shape=(out, out),
        grid_spec=pltpu.PrefetchScalarGridSpec(
            num_scalar_prefetch=2,
            grid=(1,),
            in_specs=[whole(x.shape), pl.BlockSpec(memory_space=pltpu.HBM)],
            out_specs=(whole(out.shape), whole(out.shape)),
            scratch_shapes=[
                pltpu.VMEM((capacity + slots, 2 * units), f32),
                pltpu.VMEM((experts, 2, features, units), bf16),
                pltpu.SemaphoreType.DMA((experts, 2)),
            ],
        ),
        compiler_params=params(40),
        cost_estimate=pl.CostEstimate(
            flops=4 * experts * slots * features * units,
            bytes_accessed=experts * features * units * 4 + out.size * 4,
            transcendentals=0,
        ),
        name="gate_up",
    )(me, base, x, w_gate_up)


def exchange(x, k, parts):
    return lax.ppermute(x, "gy", [(i, i ^ k) for i in range(parts)])


def place_rows(acts, firsts, names, me, scr):
    each = acts[0].shape[1]
    capacity = 2 * acts[0].shape[0] * each
    scr[capacity:, :] = jnp.zeros((scr.shape[0] - capacity, scr.shape[1]), f32)
    for ref, first, ns in zip(acts, firsts, names):
        lanes = slice(first - firsts[0], first - firsts[0] + ref.shape[2])
        for i, n in enumerate(ns):
            at = jnp.bitwise_xor(me, n) * each
            scr[pl.ds(pl.multiple_of(at, ALIGN), each), lanes] = ref[i].astype(f32)


def expert_products(base_s, w_ref, scr, first, slots, store):
    experts = w_ref.shape[0]
    lanes = slice(first, first + scr.shape[1])
    unroll = min(UNROLL, experts)

    def visit(step, carry):
        these = [step * unroll + i for i in range(unroll)]
        products = [
            lax.dot_general(
                scr[pl.ds(pl.multiple_of(base_s[e], ALIGN), slots), :].astype(bf16),
                w_ref[e, :, lanes],
                (((1,), (1,)), ((), ())),
                preferred_element_type=f32,
            )
            for e in these
        ]
        at = [pl.ds(pl.multiple_of(e * slots, 16), slots) for e in these]
        store(at, products)
        return carry

    lax.fori_loop(0, experts // unroll, visit, 0)


def down_early_kernel(firsts, names, me_s, base_s, *refs):
    acts = refs[: len(names)]
    w_ref, out_ref, scr = refs[len(names) :]
    slots = out_ref.shape[0] // w_ref.shape[0]
    place_rows(acts, firsts, names, me_s[0], scr)

    def store(at, products):
        for rows, product in zip(at, products):
            out_ref[rows, :] = product

    expert_products(base_s, w_ref, scr, firsts[0], slots, store)


def down_early(pieces, w_down_t, base, me, total_slots):
    experts, features, _ = w_down_t.shape
    firsts, acts, names = [list(column) for column in zip(*pieces)]
    capacity = 2 * acts[0].shape[0] * acts[0].shape[1]
    width = firsts[-1] + acts[-1].shape[2] - firsts[0]
    return pl.pallas_call(
        functools.partial(down_early_kernel, firsts, names),
        out_shape=jax.ShapeDtypeStruct((total_slots, features), f32),
        grid_spec=pltpu.PrefetchScalarGridSpec(
            num_scalar_prefetch=2,
            grid=(1,),
            in_specs=[whole(a.shape) for a in acts] + [pl.BlockSpec(memory_space=pltpu.VMEM)],
            out_specs=whole((total_slots, features)),
            scratch_shapes=[pltpu.VMEM((capacity + total_slots // experts, width), f32)],
        ),
        compiler_params=params(14),
        cost_estimate=pl.CostEstimate(
            flops=2 * total_slots * width * features,
            bytes_accessed=experts * features * width * 2,
            transcendentals=0,
        ),
        name="down_early",
    )(me, base, *acts, w_down_t)


def down_kernel(firsts, names, me_s, base_s, *refs):
    acts = refs[: len(names)]
    early_ref, high_ref, low_ref, w_ref = refs[len(names) : len(names) + 4]
    outs = refs[len(names) + 4 : -3]
    scr, rows_scr, total_scr = refs[-3:]
    slots = early_ref.shape[0] // w_ref.shape[0]
    place_rows(acts, firsts, names, me_s[0], scr)

    def store(at, products):
        sums = [early_ref[rows, :] + product for rows, product in zip(at, products)]
        for rows, product in zip(at, sums):
            rows_scr[rows, :] = product.astype(bf16)

    expert_products(base_s, w_ref, scr, firsts[0], slots, store)
    rows = rows_scr[...]
    total_scr[...] = jnp.dot(high_ref[...], rows, preferred_element_type=f32) + jnp.dot(
        low_ref[...], rows, preferred_element_type=f32
    )
    each = outs[0].shape[0]
    for k, out_ref in enumerate(outs):
        at = jnp.bitwise_xor(me_s[1], k) * each
        out_ref[...] = total_scr[pl.ds(pl.multiple_of(at, ALIGN), each), :]


def down(pieces, w_down_t, base, me, early, high, low):
    experts, features, _ = w_down_t.shape
    firsts, acts, names = [list(column) for column in zip(*pieces)]
    capacity = 2 * acts[0].shape[0] * acts[0].shape[1]
    slots = high.shape[1] // experts
    num_gx = E // experts
    each = high.shape[0] // num_gx
    return pl.pallas_call(
        functools.partial(down_kernel, firsts, names),
        out_shape=[jax.ShapeDtypeStruct((each, features), f32)] * num_gx,
        grid_spec=pltpu.PrefetchScalarGridSpec(
            num_scalar_prefetch=2,
            grid=(1,),
            in_specs=[whole(a.shape) for a in acts]
            + [whole(early.shape), whole(high.shape), whole(low.shape)]
            + [pl.BlockSpec(memory_space=pltpu.VMEM)],
            out_specs=[whole((each, features))] * num_gx,
            scratch_shapes=[
                pltpu.VMEM((capacity + slots, acts[0].shape[2]), f32),
                pltpu.VMEM((experts * slots, features), bf16),
                pltpu.VMEM((high.shape[0], features), f32),
            ],
        ),
        compiler_params=params(14),
        name="down",
    )(me, base, *acts, early, high, low, w_down_t)


def plan_kernel(rank_ref, weight_ref, high_ref, low_ref):
    requests, experts = rank_ref.shape
    slots = high_ref.shape[1] // experts
    rank = rank_ref[...].astype(f32).astype(bf16)
    weight = weight_ref[...]
    weight_high = weight.astype(bf16)
    weight_low = (weight - weight_high.astype(f32)).astype(bf16)
    expert = lax.broadcasted_iota(jnp.int32, (experts, experts * slots), 0)
    column = lax.broadcasted_iota(jnp.int32, (experts, experts * slots), 1)
    spread = ((column >= expert * slots) & (column < (expert + 1) * slots)).astype(f32).astype(bf16)
    offset = jnp.sum(jnp.where(column >= expert * slots, 1, 0), axis=0, keepdims=True) - 1
    slot = column[0:1] - offset * slots

    def over(x):
        return jnp.dot(x, spread, preferred_element_type=f32)

    here = over(rank).astype(jnp.int32) == slot
    high_ref[...] = jnp.where(here, over(weight_high), 0.0).astype(bf16)
    low_ref[...] = jnp.where(here, over(weight_low), 0.0).astype(bf16)


def plan(rank, weight, slots):
    out = jax.ShapeDtypeStruct((rank.shape[0], rank.shape[1] * slots), bf16)
    return pl.pallas_call(
        plan_kernel, out_shape=(out, out), compiler_params=params(6), name="plan"
    )(rank, weight)


def experts_part(capacity, x, square, w_gate_up, w_down_t, base, place, high, low, me, parts):
    hidden_units = w_down_t.shape[2]
    widths = [hidden_units * share // sum(SHARES) for share in SHARES]
    rows = capacity // parts
    here = me[0] * rows + lax.iota(jnp.int32, rows)
    mine = jnp.any(place[None] == here[:, None, None], axis=2)
    bits = [1 << i for i in range(parts.bit_length() - 1)]
    last_token = [square]
    squares = [square]
    chunks = [dict(units=w, first=sum(widths[:i])) for i, w in enumerate(widths)]

    def after(*values):
        return lax.optimization_barrier((*values, last_token[0]))[:-1]

    def send(value, k):
        last_token[0] = value
        return exchange(value, k, parts)

    def add_squares():
        done = len(squares) - 1
        if done < len(bits):
            (value,) = after(squares[-1])
            squares.append(value + send(value, bits[::-1][done]))

    places = [0]
    for k in bits[:0:-1]:
        places = places + [n ^ k for n in places]

    def start(state):
        (ordered,) = after(base)
        keep, away = gate_up(
            x, w_gate_up, ordered, me, capacity, parts, state["first"], state["units"], places, bits[0]
        )
        state.update(total=keep, got=send(away, bits[0]))

    def fold(k):
        def run(state):
            total, got = after(state["total"], state["got"])
            half = got.shape[0] // 2
            rest = (total[half:].astype(f32) + got[half:].astype(f32)).astype(bf16)
            state.update(
                total=total[:half].astype(f32) + got[:half].astype(f32), got=send(rest, k)
            )

        return run

    def activate(state):
        while len(squares) <= len(bits):
            add_squares()
        total, got = after(state["total"], state["got"])
        inv = lax.rsqrt(squares[-1].reshape(-1) / D + EPSILON)
        scale = jnp.sum(jnp.where(mine, inv[None, :], 0.0), axis=1)[:, None]
        both = total[0].astype(f32) + got[0].astype(f32)
        units = state["units"]
        gate = both[:, :units] * scale
        up = both[:, units:] * scale
        act = (jax.nn.silu(gate) * up).astype(bf16)[None]
        state.update(left=act, right=send(act, bits[-1]), names=[0], last=bits[-1])

    def spread(k):
        def run(state):
            left, right = after(state["left"], state["right"])
            both = jnp.concatenate([left, right], axis=0)
            names = state["names"] + [n ^ state["last"] for n in state["names"]]
            state.update(left=both, right=send(both, k), names=names, last=k)

        return run

    stages = [start] + [fold(k) for k in bits[1:]] + [activate] + [spread(k) for k in bits[-2::-1]]
    for slot in range(len(chunks) + len(stages) - 1):
        for i, stage in enumerate(stages):
            if 0 <= slot - i < len(chunks):
                stage(chunks[slot - i])
        add_squares()
    pieces = []
    for state in chunks:
        other = [n ^ state["last"] for n in state["names"]]
        pieces.append((state["first"], state["left"], state["names"]))
        pieces.append((state["first"], state["right"], other))
    (ordered,) = after(base)
    early = down_early(pieces[:-2], w_down_t, ordered, me, high.shape[1])
    return down(pieces[-2:], w_down_t, base, me, early, high, low)


def out_kernel(me_s, *refs):
    pieces, (w_ref, r_ref, o_ref, scr) = refs[:-4], refs[-4:]
    rows = pieces[0].shape[0]
    for k, ref in enumerate(pieces):
        at = jnp.bitwise_xor(me_s[0] // 2, k) * rows
        scr[pl.ds(pl.multiple_of(at, ALIGN), rows), :] = ref[...].astype(f32)
    projected = lax.dot_general(
        scr[...].astype(bf16), w_ref[...], (((1,), (1,)), ((), ())), preferred_element_type=f32
    )
    o_ref[...] = (r_ref[...].astype(f32) + projected).astype(bf16)


def project(pieces, out_weight, residual, me):
    return pl.pallas_call(
        out_kernel,
        out_shape=jax.ShapeDtypeStruct(residual.shape, bf16),
        grid_spec=pltpu.PrefetchScalarGridSpec(
            num_scalar_prefetch=1,
            grid=(1,),
            in_specs=[whole(p.shape) for p in pieces]
            + [whole(out_weight.shape), whole(residual.shape)],
            out_specs=whole(residual.shape),
            scratch_shapes=[pltpu.VMEM((residual.shape[0], pieces[0].shape[1]), f32)],
        ),
        compiler_params=params(8),
        name="project",
    )(me, *pieces, out_weight, residual)


def shards(
    queries,
    token_key_value,
    group_cached_keys,
    group_cached_values,
    owners,
    out_weight,
    residual,
    norm_gain,
    expert_ids,
    gate_logits,
    w_gate_up,
    w_down,
):
    rows = queries.shape[0]
    parts = lax.axis_size("gy")
    num_gx = lax.axis_size("gx")
    me_y = lax.axis_index("gy")
    me_x = lax.axis_index("gx")
    me = jnp.stack([me_y, me_x]).astype(jnp.int32)
    each = rows // parts
    slots = -(-(num_gx * CAPS + ALIGN - 1) // 16) * 16
    local = w_gate_up.shape[0]

    part = attend_local(queries, group_cached_keys, group_cached_values, owners, parts)
    part = lax.all_to_all(part, "gy", 0, 0)
    attention = merge(
        part,
        lax.dynamic_slice_in_dim(queries, me_y * each, each, 0),
        lax.dynamic_slice_in_dim(token_key_value, me_y * each, each, 0),
    )
    pairs = [[i, i + 1] for i in range(0, parts, 2)]
    attention = lax.all_gather(attention, "gy", axis=0, tiled=True, axis_index_groups=pairs)
    pieces = [attention] + [exchange(attention, 2 * k, parts) for k in range(1, parts // 2)]
    hidden = project(pieces, out_weight.T, residual, me)
    hidden_all = lax.all_gather(hidden, "gx", axis=0, tiled=True)

    mixing = jax.nn.softmax(gate_logits, axis=-1)
    rank, place, weight, base, needed = routing(expert_ids, mixing, num_gx, me_x)
    high, low = plan(rank, weight, slots)
    x, square = dispatch(hidden_all, norm_gain, rank.T, slots)

    capacity = local * num_gx * CAPS
    sizes = [c for c in (448, 512) if c < capacity and c % (ALIGN * parts) == 0] + [capacity]
    branch = sum((needed > c).astype(jnp.int32) for c in sizes[:-1])
    operands = (
        x,
        square[0].reshape(-1, 128),
        w_gate_up,
        jnp.swapaxes(w_down, 1, 2),
        base,
        place,
        high,
        low,
        me,
    )
    routed = lax.switch(
        branch,
        [lambda *o, c=c: experts_part(c, *o, parts=parts) for c in sizes],
        *operands,
    )
    total = hidden.astype(f32) + routed[0]
    for k in range(num_gx - 1, 0, -1):
        total = total + lax.ppermute(routed[k], "gx", [(i, i ^ k) for i in range(num_gx)])
    return total


def solution(mesh):
    placed = (
        P("gx", None),
        P("gx", None),
        P("gx", "gy", None),
        P("gx", "gy", None),
        P("gx", "gy"),
        P(None, "gy"),
        P("gx", "gy"),
        P("gy"),
        P(),
        P(),
        P("gx", "gy", None),
        P("gx", None, "gy"),
    )
    return jax.shard_map(
        shards, mesh=mesh, in_specs=placed, out_specs=P("gx", "gy"), check_vma=False
    )
```

```python
import functools

import jax
import jax.numpy as jnp
from jax import lax
from jax.experimental import pallas as pl
from jax.experimental.pallas import tpu as pltpu
from jax.sharding import PartitionSpec as P

D = 2560
QUERY_HEADS = 20
KEY_VALUE_HEADS = 4
HEAD_SIZE = 128
GROUP = QUERY_HEADS // KEY_VALUE_HEADS
E = 64
TOPK = 6
CAPS = 12

LOWEST = -1e30
EPSILON = 1e-05
SCALING = HEAD_SIZE ** (-0.5)
BLOCK = 1024
ROWS = 16
ALIGN = 8
SHARES = (3, 3, 3, 3)
JOINED = ()
TURNED = ()
YFIRST = (1, 3)
UNROLL = 4

f32 = jnp.float32
bf16 = jnp.bfloat16
MIB = 1024 * 1024


def params(mib):
    return pltpu.CompilerParams(vmem_limit_bytes=mib * MIB)


def whole(shape):
    return pl.BlockSpec(shape, lambda *_: (0,) * len(shape))


def attend_kernel(
    owner_s, q_ref, own_ref, k_hbm, v_hbm, out_ref, k_scr, v_scr, q_scr, m_scr, l_scr, acc_scr, sem
):
    groups = q_scr.shape[0]
    blocks = sem.shape[1]
    block = k_scr.shape[0] // blocks

    def copies(b):
        rows = pl.ds(b * block, block)
        return (
            pltpu.make_async_copy(k_hbm.at[0, rows], k_scr.at[rows], sem.at[0, b]),
            pltpu.make_async_copy(v_hbm.at[0, rows], v_scr.at[rows], sem.at[1, b]),
        )

    for b in range(blocks):
        for copy in copies(b):
            copy.start()
    for rg in range(groups):
        for c in range(KEY_VALUE_HEADS):
            for g in range(GROUP):
                h = c * GROUP + g
                q_scr[rg, c, g * ROWS : (g + 1) * ROWS, :] = q_ref[
                    rg * ROWS : (rg + 1) * ROWS, h * HEAD_SIZE : (h + 1) * HEAD_SIZE
                ]
    m_scr[...] = jnp.full(m_scr.shape, LOWEST, f32)
    l_scr[...] = jnp.zeros(l_scr.shape, f32)
    acc_scr[...] = jnp.zeros(acc_scr.shape, f32)
    heads = range(KEY_VALUE_HEADS)
    lanes = [slice(c * HEAD_SIZE, (c + 1) * HEAD_SIZE) for c in heads]

    def walk(b, carry):
        for copy in copies(b):
            copy.wait()
        at = pl.multiple_of(b * block, block)
        rows = pl.ds(at, block)
        owner = own_ref[0:1, rows]

        def visit(rg, carry):
            ids = rg * ROWS + lax.broadcasted_iota(jnp.int32, (ROWS, block), 0)
            member = owner == ids
            states = [(m_scr[rg, c], l_scr[rg, c], acc_scr[rg, c]) for c in heads]
            scores = [
                lax.dot_general(
                    q_scr[rg, c],
                    k_scr[rows, lanes[c]],
                    (((1,), (1,)), ((), ())),
                    preferred_element_type=f32,
                )
                * SCALING
                for c in heads
            ]
            results = []
            for c in heads:
                s = jnp.where(member[None], scores[c].reshape(GROUP, ROWS, block), LOWEST)
                s = s.reshape(GROUP * ROWS, block)
                m_old, l_old, acc_old = states[c]
                m_new = jnp.maximum(m_old, jnp.max(s, axis=1, keepdims=True))
                alpha = jnp.exp(m_old - m_new)
                p = jnp.exp(s - m_new[:, :1]).astype(bf16)
                l_new = l_old * alpha + jnp.sum(p.astype(f32), axis=1, keepdims=True)
                acc_new = acc_old * alpha + jnp.dot(
                    p, v_scr[rows, lanes[c]], preferred_element_type=f32
                )
                results.append((m_new, l_new, acc_new))
            for c in heads:
                m_scr[rg, c], l_scr[rg, c], acc_scr[rg, c] = results[c]
            return carry

        first = owner_s[at] // ROWS
        last = owner_s[at + block - 1] // ROWS
        return lax.fori_loop(first, last + 1, visit, carry)

    lax.fori_loop(0, blocks, walk, 0)

    width = QUERY_HEADS * HEAD_SIZE
    lane = lax.broadcasted_iota(jnp.int32, (ROWS, 128), 1)
    piece = lane % 3
    per = out_ref.shape[1]
    for rg in range(groups):

        def put(value, lanes):
            if per >= ROWS:
                at = rg * ROWS
                out_ref[at // per, at % per : at % per + ROWS, lanes] = value.astype(bf16)
            else:
                for i in range(ROWS // per):
                    out_ref[(rg * ROWS) // per + i, :, lanes] = value[
                        i * per : (i + 1) * per
                    ].astype(bf16)

        tail = jnp.zeros((ROWS, 128), f32)
        for c in heads:
            for g in range(GROUP):
                h = c * GROUP + g
                rows = slice(g * ROWS, (g + 1) * ROWS)
                m = m_scr[rg, c, rows, :]
                l = l_scr[rg, c, rows, :]
                tail = jnp.where(lane // 6 == h, jnp.where(lane % 6 < 3, m, l), tail)
                put(
                    acc_scr[rg, c, rows, :] / jnp.maximum(l, 1e-30),
                    slice(h * HEAD_SIZE, (h + 1) * HEAD_SIZE),
                )
        high = tail.astype(bf16).astype(f32)
        rest = tail - high
        middle = rest.astype(bf16).astype(f32)
        low = (rest - middle).astype(bf16).astype(f32)
        put(
            jnp.where(piece == 0, high, jnp.where(piece == 1, middle, low)),
            slice(width, width + 128),
        )


def attend_local(queries, keys, values, owners, parts):
    rows, width = queries.shape
    positions, kv = keys.shape[1:]
    block = min(BLOCK, positions)
    groups = rows // ROWS
    state = (groups, KEY_VALUE_HEADS, GROUP * ROWS, 128)
    out = jax.ShapeDtypeStruct((parts, rows // parts, width + 128), bf16)
    return pl.pallas_call(
        attend_kernel,
        out_shape=out,
        grid_spec=pltpu.PrefetchScalarGridSpec(
            num_scalar_prefetch=1,
            grid=(1,),
            in_specs=[
                whole((rows, width)),
                whole((1, positions)),
                pl.BlockSpec(memory_space=pltpu.HBM),
                pl.BlockSpec(memory_space=pltpu.HBM),
            ],
            out_specs=whole(out.shape),
            scratch_shapes=[
                pltpu.VMEM((positions, kv), bf16),
                pltpu.VMEM((positions, kv), bf16),
                pltpu.VMEM((groups, KEY_VALUE_HEADS, GROUP * ROWS, HEAD_SIZE), bf16),
                pltpu.VMEM(state, f32),
                pltpu.VMEM(state, f32),
                pltpu.VMEM(state, f32),
                pltpu.SemaphoreType.DMA((2, positions // block)),
            ],
        ),
        compiler_params=params(56),
        name="attend",
    )(owners.reshape(-1), queries, owners, keys, values)


def merge_kernel(part_ref, q_ref, kv_ref, out_ref):
    parts, rows, _ = part_ref.shape
    width = QUERY_HEADS * HEAD_SIZE
    kv = KEY_VALUE_HEADS * HEAD_SIZE
    source = lax.broadcasted_iota(jnp.int32, (128, 256), 0)
    target = lax.broadcasted_iota(jnp.int32, (128, 256), 1)
    wanted = (target % 128) * 6 + (target // 128) * 3
    pick = jnp.where(
        (source >= wanted) & (source < wanted + 3) & (target % 128 < QUERY_HEADS), 1.0, 0.0
    ).astype(bf16)
    lane = lax.broadcasted_iota(jnp.int32, (rows, 128), 1)
    own = jnp.zeros((rows, 128), f32)
    for h in range(QUERY_HEADS):
        c = h // GROUP
        product = q_ref[:, h * HEAD_SIZE : (h + 1) * HEAD_SIZE].astype(f32) * kv_ref[
            :, c * HEAD_SIZE : (c + 1) * HEAD_SIZE
        ].astype(f32)
        own = jnp.where(lane == h, jnp.sum(product, axis=1, keepdims=True) * SCALING, own)
    maxima, sums = [], []
    peak = own
    for j in range(parts):
        both = jnp.dot(part_ref[j, :, width:], pick, preferred_element_type=f32)
        maxima.append(both[:, :128])
        sums.append(both[:, 128:])
        peak = jnp.maximum(peak, both[:, :128])
    own_prob = jnp.exp(own - peak).astype(bf16).astype(f32)
    weights = [l * jnp.exp(m - peak) for m, l in zip(maxima, sums)]
    den = own_prob
    for w in weights:
        den = den + w
    own_prob = own_prob / den
    weights = [w / den for w in weights]
    for h in range(QUERY_HEADS):
        c = h // GROUP
        lanes = slice(h * HEAD_SIZE, (h + 1) * HEAD_SIZE)
        acc = own_prob[:, h : h + 1] * kv_ref[
            :, kv + c * HEAD_SIZE : kv + (c + 1) * HEAD_SIZE
        ].astype(f32)
        for j in range(parts):
            acc = acc + weights[j][:, h : h + 1] * part_ref[j, :, lanes].astype(f32)
        out_ref[:, lanes] = acc.astype(bf16)


def merge(part, queries, token_key_value):
    return pl.pallas_call(
        merge_kernel,
        out_shape=jax.ShapeDtypeStruct(queries.shape, bf16),
        compiler_params=params(6),
        name="merge",
    )(part, queries, token_key_value)


def routing(expert_ids, mixing, num_gx, group_index):
    local = E // num_gx
    hit = expert_ids[:, :, None] == lax.iota(jnp.int32, E)
    named = jnp.any(hit, axis=1)
    counts = jnp.sum(named.astype(jnp.int32), axis=0).reshape(num_gx, local)
    needed = jnp.max(jnp.sum(counts, axis=1))
    earlier = lax.iota(jnp.int32, local)[:, None] < lax.iota(jnp.int32, local)[None, :]
    starts = jnp.sum(jnp.where(earlier[None], counts[:, :, None], 0), axis=1)
    mine = group_index * local + lax.iota(jnp.int32, local)
    hit_mine = expert_ids[:, :, None] == mine
    mine_named = jnp.any(hit_mine, axis=1)
    weight = jnp.sum(jnp.where(hit_mine, mixing[:, :, None], 0.0), axis=1)
    requests = expert_ids.shape[0]
    before = (lax.iota(jnp.int32, requests)[None, :] < lax.iota(jnp.int32, requests)[:, None])
    rank = jnp.dot(
        before.astype(bf16), mine_named.astype(bf16), preferred_element_type=f32
    ).astype(jnp.int32)
    start = lax.dynamic_index_in_dim(starts, group_index, 0, False)
    place = jnp.where(mine_named, rank + start[None, :], -1)
    base = start // ALIGN * ALIGN
    rank = jnp.where(mine_named, place - base[None, :], -1)
    return rank, place, weight, base, needed


def dispatch_kernel(h_ref, gain_ref, rank_ref, x_ref, square_ref):
    slots = x_ref.shape[1]
    h = h_ref[...].astype(f32)
    square_ref[...] = lax.dot_general(
        jnp.ones((8, h.shape[1]), f32),
        h * h,
        (((1,), (1,)), ((), ())),
        precision=lax.Precision.HIGHEST,
        preferred_element_type=f32,
    )
    scaled = (h * gain_ref[...].astype(f32)).astype(bf16)
    slot = lax.broadcasted_iota(jnp.int32, (slots, h.shape[0]), 0)
    for e in range(x_ref.shape[0]):
        pick = (rank_ref[e : e + 1, :] == slot).astype(f32).astype(bf16)
        x_ref[e] = jnp.dot(pick, scaled, preferred_element_type=f32).astype(bf16)


def dispatch(hidden_all, gain, rank_t, slots):
    requests, features = hidden_all.shape
    return pl.pallas_call(
        dispatch_kernel,
        out_shape=(
            jax.ShapeDtypeStruct((rank_t.shape[0], slots, features), bf16),
            jax.ShapeDtypeStruct((8, requests), f32),
        ),
        compiler_params=params(6),
        name="dispatch",
    )(hidden_all, gain.reshape(1, -1), rank_t)


def gate_up_kernel(names, bit, first, hidden_units, me_s, base_s, x_ref, w_hbm, keep_ref, send_ref, scr, buf, sem):
    experts, slots, _ = x_ref.shape
    units = buf.shape[3]

    def copies(e):
        return [
            pltpu.make_async_copy(
                w_hbm.at[e, :, pl.ds(half * hidden_units + first, units)],
                buf.at[e, half],
                sem.at[e, half],
            )
            for half in range(2)
        ]

    for e in range(experts):
        for copy in copies(e):
            copy.start()
    scr[...] = jnp.zeros(scr.shape, f32)
    unroll = min(UNROLL, experts)

    def visit(step, carry):
        these = [step * unroll + i for i in range(unroll)]
        for e in these:
            for copy in copies(e):
                copy.wait()
        products = [
            [jnp.dot(x_ref[e], buf[e, half], preferred_element_type=f32) for half in range(2)]
            for e in these
        ]
        for e, pair in zip(these, products):
            rows = pl.ds(pl.multiple_of(base_s[e], ALIGN), slots)
            for half in range(2):
                scr[rows, half * units : (half + 1) * units] += pair[half]
        return carry

    lax.fori_loop(0, experts // unroll, visit, 0)
    each = keep_ref.shape[1]
    me = me_s[0]
    for i, name in enumerate(names):
        at = jnp.bitwise_xor(me, name) * each
        keep_ref[i] = scr[pl.ds(pl.multiple_of(at, ALIGN), each), :].astype(bf16)
        at = jnp.bitwise_xor(me, name ^ bit) * each
        send_ref[i] = scr[pl.ds(pl.multiple_of(at, ALIGN), each), :].astype(bf16)


def gate_up(x, w_gate_up, base, me, capacity, parts, first, units, names, bit):
    experts, slots, features = x.shape
    hidden_units = w_gate_up.shape[2] // 2
    out = jax.ShapeDtypeStruct((parts // 2, capacity // parts, 2 * units), bf16)
    return pl.pallas_call(
        functools.partial(gate_up_kernel, names, bit, first, hidden_units),
        out_shape=(out, out),
        grid_spec=pltpu.PrefetchScalarGridSpec(
            num_scalar_prefetch=2,
            grid=(1,),
            in_specs=[whole(x.shape), pl.BlockSpec(memory_space=pltpu.HBM)],
            out_specs=(whole(out.shape), whole(out.shape)),
            scratch_shapes=[
                pltpu.VMEM((capacity + slots, 2 * units), f32),
                pltpu.VMEM((experts, 2, features, units), bf16),
                pltpu.SemaphoreType.DMA((experts, 2)),
            ],
        ),
        compiler_params=params(40),
        cost_estimate=pl.CostEstimate(
            flops=4 * experts * slots * features * units,
            bytes_accessed=experts * features * units * 4 + out.size * 4,
            transcendentals=0,
        ),
        name="gate_up",
    )(me, base, x, w_gate_up)


def exchange(x, k, parts):
    return lax.ppermute(x, "gy", [(i, i ^ k) for i in range(parts)])


def place_rows(acts, firsts, names, me, scr):
    each = acts[0].shape[1]
    capacity = 2 * acts[0].shape[0] * each
    scr[capacity:, :] = jnp.zeros((scr.shape[0] - capacity, scr.shape[1]), f32)
    for ref, first, ns in zip(acts, firsts, names):
        lanes = slice(first - firsts[0], first - firsts[0] + ref.shape[2])
        for i, n in enumerate(ns):
            at = jnp.bitwise_xor(me, n) * each
            scr[pl.ds(pl.multiple_of(at, ALIGN), each), lanes] = ref[i].astype(f32)


def expert_products(base_s, w_ref, scr, first, slots, store):
    experts = w_ref.shape[0]
    lanes = slice(first, first + scr.shape[1])
    unroll = min(UNROLL, experts)

    def visit(step, carry):
        these = [step * unroll + i for i in range(unroll)]
        products = [
            lax.dot_general(
                scr[pl.ds(pl.multiple_of(base_s[e], ALIGN), slots), :].astype(bf16),
                w_ref[e, :, lanes],
                (((1,), (1,)), ((), ())),
                preferred_element_type=f32,
            )
            for e in these
        ]
        at = [pl.ds(pl.multiple_of(e * slots, 16), slots) for e in these]
        store(at, products)
        return carry

    lax.fori_loop(0, experts // unroll, visit, 0)


def down_early_kernel(firsts, names, me_s, base_s, *refs):
    acts = refs[: len(names)]
    w_ref, out_ref, scr = refs[len(names) :]
    slots = out_ref.shape[0] // w_ref.shape[0]
    place_rows(acts, firsts, names, me_s[0], scr)

    def store(at, products):
        for rows, product in zip(at, products):
            out_ref[rows, :] = product

    expert_products(base_s, w_ref, scr, firsts[0], slots, store)


def down_early(pieces, w_down_t, base, me, total_slots):
    experts, features, _ = w_down_t.shape
    firsts, acts, names = [list(column) for column in zip(*pieces)]
    capacity = 2 * acts[0].shape[0] * acts[0].shape[1]
    width = firsts[-1] + acts[-1].shape[2] - firsts[0]
    return pl.pallas_call(
        functools.partial(down_early_kernel, firsts, names),
        out_shape=jax.ShapeDtypeStruct((total_slots, features), f32),
        grid_spec=pltpu.PrefetchScalarGridSpec(
            num_scalar_prefetch=2,
            grid=(1,),
            in_specs=[whole(a.shape) for a in acts] + [pl.BlockSpec(memory_space=pltpu.VMEM)],
            out_specs=whole((total_slots, features)),
            scratch_shapes=[pltpu.VMEM((capacity + total_slots // experts, width), f32)],
        ),
        compiler_params=params(14),
        cost_estimate=pl.CostEstimate(
            flops=2 * total_slots * width * features,
            bytes_accessed=experts * features * width * 2,
            transcendentals=0,
        ),
        name="down_early",
    )(me, base, *acts, w_down_t)


def down_kernel(firsts, names, me_s, base_s, *refs):
    acts = refs[: len(names)]
    early_ref, high_ref, low_ref, w_ref = refs[len(names) : len(names) + 4]
    outs = refs[len(names) + 4 : -3]
    scr, rows_scr, total_scr = refs[-3:]
    slots = early_ref.shape[0] // w_ref.shape[0]
    place_rows(acts, firsts, names, me_s[0], scr)

    def store(at, products):
        sums = [early_ref[rows, :] + product for rows, product in zip(at, products)]
        for rows, product in zip(at, sums):
            rows_scr[rows, :] = product.astype(bf16)

    expert_products(base_s, w_ref, scr, firsts[0], slots, store)
    rows = rows_scr[...]
    total_scr[...] = jnp.dot(high_ref[...], rows, preferred_element_type=f32) + jnp.dot(
        low_ref[...], rows, preferred_element_type=f32
    )
    each = outs[0].shape[0]
    for k, out_ref in enumerate(outs):
        at = jnp.bitwise_xor(me_s[1], k) * each
        out_ref[...] = total_scr[pl.ds(pl.multiple_of(at, ALIGN), each), :]


def down(pieces, w_down_t, base, me, early, high, low):
    experts, features, _ = w_down_t.shape
    firsts, acts, names = [list(column) for column in zip(*pieces)]
    capacity = 2 * acts[0].shape[0] * acts[0].shape[1]
    slots = high.shape[1] // experts
    num_gx = E // experts
    each = high.shape[0] // num_gx
    return pl.pallas_call(
        functools.partial(down_kernel, firsts, names),
        out_shape=[jax.ShapeDtypeStruct((each, features), f32)] * num_gx,
        grid_spec=pltpu.PrefetchScalarGridSpec(
            num_scalar_prefetch=2,
            grid=(1,),
            in_specs=[whole(a.shape) for a in acts]
            + [whole(early.shape), whole(high.shape), whole(low.shape)]
            + [pl.BlockSpec(memory_space=pltpu.VMEM)],
            out_specs=[whole((each, features))] * num_gx,
            scratch_shapes=[
                pltpu.VMEM((capacity + slots, acts[0].shape[2]), f32),
                pltpu.VMEM((experts * slots, features), bf16),
                pltpu.VMEM((high.shape[0], features), f32),
            ],
        ),
        compiler_params=params(14),
        name="down",
    )(me, base, *acts, early, high, low, w_down_t)


def plan_kernel(rank_ref, weight_ref, high_ref, low_ref):
    requests, experts = rank_ref.shape
    slots = high_ref.shape[1] // experts
    rank = rank_ref[...].astype(f32).astype(bf16)
    weight = weight_ref[...]
    weight_high = weight.astype(bf16)
    weight_low = (weight - weight_high.astype(f32)).astype(bf16)
    expert = lax.broadcasted_iota(jnp.int32, (experts, experts * slots), 0)
    column = lax.broadcasted_iota(jnp.int32, (experts, experts * slots), 1)
    spread = ((column >= expert * slots) & (column < (expert + 1) * slots)).astype(f32).astype(bf16)
    offset = jnp.sum(jnp.where(column >= expert * slots, 1, 0), axis=0, keepdims=True) - 1
    slot = column[0:1] - offset * slots

    def over(x):
        return jnp.dot(x, spread, preferred_element_type=f32)

    here = over(rank).astype(jnp.int32) == slot
    high_ref[...] = jnp.where(here, over(weight_high), 0.0).astype(bf16)
    low_ref[...] = jnp.where(here, over(weight_low), 0.0).astype(bf16)


def plan(rank, weight, slots):
    out = jax.ShapeDtypeStruct((rank.shape[0], rank.shape[1] * slots), bf16)
    return pl.pallas_call(
        plan_kernel, out_shape=(out, out), compiler_params=params(6), name="plan"
    )(rank, weight)


def experts_part(capacity, x, square, w_gate_up, w_down_t, base, place, high, low, me, parts):
    hidden_units = w_down_t.shape[2]
    widths = [hidden_units * share // sum(SHARES) for share in SHARES]
    rows = capacity // parts
    here = me[0] * rows + lax.iota(jnp.int32, rows)
    mine = jnp.any(place[None] == here[:, None, None], axis=2)
    bits = [1 << i for i in range(parts.bit_length() - 1)]
    last_token = [square]
    squares = [square]
    chunks = [dict(units=w, first=sum(widths[:i])) for i, w in enumerate(widths)]

    def after(*values):
        return lax.optimization_barrier((*values, last_token[0]))[:-1]

    def send(value, k):
        last_token[0] = value
        return exchange(value, k, parts)

    def add_squares():
        done = len(squares) - 1
        if done < len(bits):
            (value,) = after(squares[-1])
            squares.append(value + send(value, bits[::-1][done]))

    for i, state in enumerate(chunks):
        order = bits[1:] + bits[:1] if i in TURNED else bits
        places = [0]
        for k in order[:0:-1]:
            places = places + [n ^ k for n in places]
        state.update(order=order, places=places, joined=i in JOINED)
        back = order[::-1]
        state.update(back=back[-1:] + back[:-1] if i in YFIRST else back)

    def start(state):
        (ordered,) = after(base)
        order = state["order"]
        keep, away = gate_up(
            x, w_gate_up, ordered, me, capacity, parts, state["first"], state["units"],
            state["places"], order[0]
        )
        state.update(total=keep, got=send(away, order[0]))

    def fold(i):
        def run(state):
            total, got = after(state["total"], state["got"])
            half = got.shape[0] // 2
            rest = (total[half:].astype(f32) + got[half:].astype(f32)).astype(bf16)
            state.update(
                total=total[:half].astype(f32) + got[:half].astype(f32),
                got=send(rest, state["order"][i]),
            )

        return run

    waiting = []

    def activate(state):
        while len(squares) <= len(bits):
            add_squares()
        total, got = after(state["total"], state["got"])
        inv = lax.rsqrt(squares[-1].reshape(-1) / D + EPSILON)
        scale = jnp.sum(jnp.where(mine, inv[None, :], 0.0), axis=1)[:, None]
        both = total[0].astype(f32) + got[0].astype(f32)
        units = state["units"]
        gate = both[:, :units] * scale
        up = both[:, units:] * scale
        act = (jax.nn.silu(gate) * up).astype(bf16)[None]
        waiting.append((state["first"], act))
        if state["joined"]:
            return
        state.update(first=waiting[0][0])
        act = jnp.concatenate([a for _, a in waiting], axis=2)
        waiting.clear()
        last = state["back"][0]
        state.update(left=act, right=send(act, last), names=[0], last=last)

    def spread(i):
        def run(state):
            if state["joined"]:
                return
            k = state["back"][i]
            left, right = after(state["left"], state["right"])
            both = jnp.concatenate([left, right], axis=0)
            names = state["names"] + [n ^ state["last"] for n in state["names"]]
            state.update(left=both, right=send(both, k), names=names, last=k)

        return run

    steps = range(len(bits))
    stages = [start] + [fold(i) for i in steps[1:]] + [activate] + [spread(i) for i in steps[1:]]
    for slot in range(len(chunks) + len(stages) - 1):
        for i, stage in enumerate(stages):
            if 0 <= slot - i < len(chunks):
                stage(chunks[slot - i])
        add_squares()
    pieces = []
    for state in chunks:
        if state["joined"]:
            continue
        other = [n ^ state["last"] for n in state["names"]]
        pieces.append((state["first"], state["left"], state["names"]))
        pieces.append((state["first"], state["right"], other))
    (ordered,) = after(base)
    early = down_early(pieces[:-2], w_down_t, ordered, me, high.shape[1])
    return down(pieces[-2:], w_down_t, base, me, early, high, low)


def out_kernel(me_s, *refs):
    pieces, (w_ref, r_ref, o_ref, scr) = refs[:-4], refs[-4:]
    rows = pieces[0].shape[0]
    for k, ref in enumerate(pieces):
        at = jnp.bitwise_xor(me_s[0] // 2, k) * rows
        scr[pl.ds(pl.multiple_of(at, ALIGN), rows), :] = ref[...].astype(f32)
    projected = lax.dot_general(
        scr[...].astype(bf16), w_ref[...], (((1,), (1,)), ((), ())), preferred_element_type=f32
    )
    o_ref[...] = (r_ref[...].astype(f32) + projected).astype(bf16)


def project(pieces, out_weight, residual, me):
    return pl.pallas_call(
        out_kernel,
        out_shape=jax.ShapeDtypeStruct(residual.shape, bf16),
        grid_spec=pltpu.PrefetchScalarGridSpec(
            num_scalar_prefetch=1,
            grid=(1,),
            in_specs=[whole(p.shape) for p in pieces]
            + [whole(out_weight.shape), whole(residual.shape)],
            out_specs=whole(residual.shape),
            scratch_shapes=[pltpu.VMEM((residual.shape[0], pieces[0].shape[1]), f32)],
        ),
        compiler_params=params(8),
        name="project",
    )(me, *pieces, out_weight, residual)


def shards(
    queries,
    token_key_value,
    group_cached_keys,
    group_cached_values,
    owners,
    out_weight,
    residual,
    norm_gain,
    expert_ids,
    gate_logits,
    w_gate_up,
    w_down,
):
    rows = queries.shape[0]
    parts = lax.axis_size("gy")
    num_gx = lax.axis_size("gx")
    me_y = lax.axis_index("gy")
    me_x = lax.axis_index("gx")
    me = jnp.stack([me_y, me_x]).astype(jnp.int32)
    each = rows // parts
    slots = -(-(num_gx * CAPS + ALIGN - 1) // 16) * 16
    local = w_gate_up.shape[0]

    part = attend_local(queries, group_cached_keys, group_cached_values, owners, parts)
    part = lax.all_to_all(part, "gy", 0, 0)
    attention = merge(
        part,
        lax.dynamic_slice_in_dim(queries, me_y * each, each, 0),
        lax.dynamic_slice_in_dim(token_key_value, me_y * each, each, 0),
    )
    pairs = [[i, i + 1] for i in range(0, parts, 2)]
    attention = lax.all_gather(attention, "gy", axis=0, tiled=True, axis_index_groups=pairs)
    pieces = [attention] + [exchange(attention, 2 * k, parts) for k in range(1, parts // 2)]
    hidden = project(pieces, out_weight.T, residual, me)
    hidden_all = lax.all_gather(hidden, "gx", axis=0, tiled=True)

    mixing = jax.nn.softmax(gate_logits, axis=-1)
    rank, place, weight, base, needed = routing(expert_ids, mixing, num_gx, me_x)
    high, low = plan(rank, weight, slots)
    x, square = dispatch(hidden_all, norm_gain, rank.T, slots)

    capacity = local * num_gx * CAPS
    sizes = [c for c in (448, 512) if c < capacity and c % (ALIGN * parts) == 0] + [capacity]
    branch = sum((needed > c).astype(jnp.int32) for c in sizes[:-1])
    operands = (
        x,
        square[0].reshape(-1, 128),
        w_gate_up,
        jnp.swapaxes(w_down, 1, 2),
        base,
        place,
        high,
        low,
        me,
    )
    routed = lax.switch(
        branch,
        [lambda *o, c=c: experts_part(c, *o, parts=parts) for c in sizes],
        *operands,
    )
    total = hidden.astype(f32) + routed[0]
    for k in range(num_gx - 1, 0, -1):
        total = total + lax.ppermute(routed[k], "gx", [(i, i ^ k) for i in range(num_gx)])
    return total


def solution(mesh):
    placed = (
        P("gx", None),
        P("gx", None),
        P("gx", "gy", None),
        P("gx", "gy", None),
        P("gx", "gy"),
        P(None, "gy"),
        P("gx", "gy"),
        P("gy"),
        P(),
        P(),
        P("gx", "gy", None),
        P("gx", None, "gy"),
    )
    return jax.shard_map(
        shards, mesh=mesh, in_specs=placed, out_specs=P("gx", "gy"), check_vma=False
    )
```
